32 devices in a mesh: gz: 32 (over z, y, x, core).
Axes of the slice: x: 2, y: 2, z: 4, core: 2. Of those that a mesh axis runs over, the one named last changes fastest.
Arguments:
- marker_positions: float32 [4096, 3, 256], P('gz'), may hold values from 0 to 1
- marker_forces: float32 [4096, 3, 256], P('gz'), may hold values from -48 to 48
- dest_slab: int32 [4096, 1], P('gz'), may hold values from 0 to 31; in each aligned block of 128 rows (0 to 127, 128 to 255, ...) at most 8 rows name the same one
- base_cells: int32 [4096, 2], P('gz'), may hold values from 0 to 127
- fluid_source: float32 [128, 3, 128, 128], P('gz'), may hold values from -7 to 7
Outputs:
- velocity: float32 [128, 3, 128, 128], P('gz')
- marker_velocity: float32 [4096, 3, 256], P('gz')
The draws below stay inside these ranges and needn't reach their ends.
Inputs may be any that keep to these rules, and one draw needn't show every extreme that they name: `dest_slab`: among the blocks of one device no slab is named more than 8 times.
All inputs are finite; a program needn't handle non-finite values.
Results may differ from the reference program's by a relative error of at most 0.00096.
Values may be sent and summed in bfloat16 or wider, within the bound.
A program may use at most 256 MiB of HBM per device.

```python
import math
import jax
import jax.numpy as jnp
import numpy as np
from jax import lax

CELLS_XY = 128
CZ = 4
NZ = 128
BLK_DEV = 128
BLOCKS = 4096
MARK = 256
BOX = 16
CAP = 8
SWEEPS = 2
CSWEEPS = 6
N_GZ = 32


def draw_fluid_source(key, part):
    rough_key, level_key = jax.random.split(jax.random.fold_in(key, 11))
    rough = jax.random.truncated_normal(rough_key, -6.0, 6.0, (NZ, 3, CELLS_XY, CELLS_XY), jnp.float32)
    levels = jax.random.uniform(level_key, (NZ // CZ,), jnp.float32, 0.01, 0.05)
    return rough + jnp.repeat(levels, CZ)[:, None, None, None]


def with_ends(drawn, stream_key, smallest, high):
    spot = [jax.random.randint(jax.random.fold_in(stream_key, axis), (), 0, length) for axis, length in enumerate(drawn.shape)]
    main_axis = drawn.shape.index(max(drawn.shape))
    neighbour = spot[:main_axis] + [(spot[main_axis] + 1) % drawn.shape[main_axis]] + spot[main_axis + 1:]
    return drawn.at[tuple(spot)].set(smallest).at[tuple(neighbour)].set(high)


def steps_of(stream_key, shape, cuts, least, top_value):
    gain = 1.0
    for position, shards_of in cuts:
        steps = jax.random.uniform(jax.random.fold_in(jax.random.fold_in(stream_key, 6), position), (shards_of,), jnp.float32, least / len(cuts), top_value / len(cuts))
        gain = gain * jnp.repeat(jnp.exp(steps), shape[position] // shards_of).reshape((-1,) + (1,) * (len(shape) - 1 - position))
    return gain


def shared_out(own_key, own, number, rows, number_of, top, most, lean):
    sequence = jax.random.permutation(own_key, number_of)
    heavy_load, ordinary = shares(number_of, rows * top, most, lean, True), shares(number_of, rows * top, most, lean, False)
    places = jnp.arange(number_of)

    def named(tallies, offset_by):
        used = int((tallies > 0).sum())
        fixed = max(1, used // 4)
        moved = fixed + (places - fixed + offset_by * (used - fixed)) % max(1, number_of - fixed)
        return jnp.zeros((number_of,), jnp.int32).at[sequence[jnp.where(places < fixed, places, moved)]].set(jnp.asarray(tallies, jnp.int32))

    tallies = jnp.where(number % 4 == 0, named(heavy_load, number // 4), named(ordinary, number - number // 4 - 1))
    mixed = jax.random.permutation(jax.random.fold_in(own, 3), number_of)
    giver, taker = mixed[0:number_of // 2 * 2:2], mixed[1:number_of // 2 * 2:2]
    margin = jnp.minimum(tallies[giver] - 1, most - tallies[taker]) // 2
    margin = jnp.where((giver == sequence[0]) | (taker == sequence[0]) | (tallies[taker] == 0), 0, jnp.maximum(margin, 0))
    moved = jax.random.randint(jax.random.fold_in(own, 4), (number_of // 2,), 0, 1 << 20) % (margin + 1)
    tallies = tallies.at[giver].add(-moved).at[taker].add(moved)
    labels = jnp.searchsorted(jnp.cumsum(tallies), jnp.arange(rows * top), side="right").astype(jnp.int32)
    grid = labels.reshape(top, rows).T
    grid = grid[jax.random.permutation(jax.random.fold_in(own, 1), rows)]
    offset_by = jax.random.randint(jax.random.fold_in(own, 2), (rows, 1), 0, top)
    return jnp.take_along_axis(grid, (jnp.arange(top)[None, :] + offset_by) % top, axis=1)


def shares(count, total, bound, slope, full):
    loads = [(1 << 20) // math.isqrt(standing ** slope) + 1 for standing in range(1, count + 1)]
    largest = bound if full else min(bound, max(-(-total // count), total * loads[0] // sum(loads)))
    least = 1 if total - largest >= count - 1 else 0
    counts, rest = [largest] + [least] * (count - 1), total - largest - least * (count - 1)
    while rest > 0:
        movable = [i for i in range(1, count) if counts[i] < largest] or [i for i in range(1, count) if counts[i] < bound]
        whole, left = sum([loads[i] for i in movable]), rest
        for i in movable:
            more = min(bound - counts[i], max(1, left * loads[i] // whole), rest)
            counts[i] = counts[i] + more
            rest = rest - more
    return np.array(counts)


def normal_values(own_key, extent, deviation, reach, cuts=(), kind=jnp.bfloat16):
    loudness = steps_of(own_key, extent, cuts, -0.22, 0.18) if cuts else 1.0
    values = jax.random.normal(own_key, extent, jnp.float32) * deviation * loudness
    return jnp.minimum(jnp.maximum(values, -reach), reach).astype(kind)


def setup_inputs(seed: int = 0) -> dict:
    streams_of = jax.random.split(jax.random.key(seed), 6)
    marker_positions = jnp.clip(1.0 * jax.random.uniform(streams_of[0], (BLOCKS, 3, MARK), jnp.float32) ** steps_of(streams_of[0], (BLOCKS, 3, MARK), ((0, 32),), -0.2, 0.2), 0.0, 1.0)
    marker_forces = normal_values(streams_of[1], (BLOCKS, 3, MARK), 8.0, 48.0, ((0, 32),), jnp.float32)
    dest_slab_keys = jax.random.split(jax.random.fold_in(streams_of[2], 1), BLOCKS // BLK_DEV)
    dest_slab_turns = jax.random.permutation(jax.random.fold_in(streams_of[2], 3), BLOCKS // BLK_DEV)
    dest_slab = jax.vmap(lambda own, number: shared_out(jax.random.fold_in(streams_of[2], 2), own, number, BLK_DEV, N_GZ, 1, CAP, 2))(dest_slab_keys, dest_slab_turns).reshape((BLOCKS, 1))
    base_cells = with_ends(jax.random.randint(streams_of[3], (BLOCKS, 2), 0, CELLS_XY), jax.random.fold_in(streams_of[3], 1), 0, CELLS_XY - 1).astype(jnp.int32)
    fluid_source = draw_fluid_source(jax.random.fold_in(streams_of[5], 71), 0)
    return {"marker_positions": marker_positions, "marker_forces": marker_forces, "dest_slab": dest_slab, "base_cells": base_cells, "fluid_source": fluid_source}


screening = 1.0 / 64.0
relaxation = 2.0 / 3.0


def kernel_phi(offset):
    inside = jnp.abs(offset) < 2.0
    return jnp.where(inside, 0.25 * (1.0 + jnp.cos(0.5 * jnp.pi * offset)), 0.0 * offset)


def kernel_tables(positions):
    box_cells = jnp.arange(BOX, dtype=positions.dtype)
    slab_cells = jnp.arange(CZ, dtype=positions.dtype)
    across = 2.0 + (BOX - 5) * positions[:, 0, :]
    along_y = 2.0 + (BOX - 5) * positions[:, 1, :]
    height = (CZ - 1) * positions[:, 2, :]
    weight_x = kernel_phi(across[:, :, None] - box_cells)
    weight_y = kernel_phi(along_y[:, :, None] - box_cells)
    weight_z = kernel_phi(height[:, :, None] - slab_cells)
    plane_weight = (weight_x[:, :, :, None] * weight_y[:, :, None, :]).reshape(positions.shape[0], positions.shape[2], BOX * BOX)
    return weight_z, plane_weight


def build_boxes(positions, forces):
    weight_z, plane_weight = kernel_tables(positions)
    loaded = jnp.einsum('bmk,bcm->bkcm', weight_z, forces, precision=lax.Precision.HIGHEST)
    box_values = jnp.einsum('bkcm,bmq->bkcq', loaded, plane_weight, precision=lax.Precision.HIGHEST)
    return box_values.reshape(positions.shape[0], -1).astype(jnp.bfloat16)


def read_boxes(positions, box_velocity):
    weight_z, plane_weight = kernel_tables(positions)
    block_total = positions.shape[0]
    box_values = box_velocity.astype(jnp.float32).reshape(block_total, CZ, 3, BOX * BOX)
    spread = jnp.einsum('bkcq,bmq->bkcm', box_values, plane_weight, precision=lax.Precision.HIGHEST)
    return jnp.einsum('bmk,bkcm->bcm', weight_z, spread, precision=lax.Precision.HIGHEST)


def grouped(function, arrays, group_rows):
    block_total = arrays[0].shape[0]
    stacked = tuple(member.reshape((block_total // group_rows, group_rows) + member.shape[1:]) for member in arrays)
    result = lax.map(lambda pieces: function(*pieces), stacked)
    return result.reshape((block_total,) + result.shape[2:])


def box_index(target, bases):
    layer_index = target[:, None] * CZ + jnp.arange(CZ, dtype=jnp.int32)[None, :]
    column_x = (bases[:, 0:1] + jnp.arange(BOX, dtype=jnp.int32)[None, :]) % CELLS_XY
    column_y = (bases[:, 1:2] + jnp.arange(BOX, dtype=jnp.int32)[None, :]) % CELLS_XY
    component = jnp.arange(3, dtype=jnp.int32)
    return (layer_index[:, :, None, None, None], component[None, None, :, None, None],
            column_x[:, None, None, :, None], column_y[:, None, None, None, :])


def operate(solution, level_index):
    beside = jnp.roll(solution, -1, 0) + jnp.roll(solution, 1, 0)
    beside = beside + jnp.roll(solution, -1, 2) + jnp.roll(solution, 1, 2)
    beside = beside + jnp.roll(solution, -1, 3) + jnp.roll(solution, 1, 3)
    return screening * solution - 0.25 ** level_index * (beside - 6.0 * solution)


def relax_factor(level_index):
    return relaxation / (screening + 6.0 * 0.25 ** level_index)


def restrict(solution):
    shape_now = solution.shape
    folded = solution.reshape(shape_now[0] // 2, 2, shape_now[1], shape_now[2] // 2, 2, shape_now[3] // 2, 2)
    return jnp.mean(folded, axis=(1, 4, 6))


def prolong(solution):
    return jnp.repeat(jnp.repeat(jnp.repeat(solution, 2, 0), 2, 2), 2, 3)


def descend(source, level_index):
    factor = relax_factor(level_index)
    solution = factor * source
    for sweep_turn in range(SWEEPS - 1):
        solution = solution + factor * (source - operate(solution, level_index))
    return solution, source - operate(solution, level_index)


def ascend(solution, source, level_index):
    factor = relax_factor(level_index)
    for sweep_turn in range(SWEEPS):
        solution = solution + factor * (source - operate(solution, level_index))
    return solution


def coarsest(source):
    factor = relax_factor(3)
    solution = factor * source
    for sweep_turn in range(CSWEEPS - 1):
        solution = solution + factor * (source - operate(solution, 3))
    leftover = source - operate(solution, 3)
    level_mean = jnp.mean(leftover, axis=(0, 2, 3), keepdims=True)
    return solution + level_mean / screening


def reference(marker_positions, marker_forces, dest_slab, base_cells, fluid_source):
    group_rows = math.gcd(BLOCKS, 256)
    own_boxes = grouped(build_boxes, (marker_positions, marker_forces), group_rows)
    target = dest_slab[:, 0]
    group_count = BLOCKS // group_rows

    def place(grid_sum, pieces):
        group_boxes, group_target, group_base = pieces
        box_values = group_boxes.astype(jnp.float32).reshape(group_rows, CZ, 3, BOX, BOX)
        grid_sum = grid_sum.at[box_index(group_target, group_base)].add(box_values)
        return grid_sum, None

    start_grid = jnp.zeros((NZ, 3, CELLS_XY, CELLS_XY), jnp.float32)
    force_grid, unused = lax.scan(place, start_grid, (
        own_boxes.reshape(group_count, group_rows, -1),
        target.reshape(group_count, group_rows),
        base_cells.reshape(group_count, group_rows, 2)))
    source = fluid_source + force_grid
    fine_sol, fine_res = descend(source, 0)
    middle_rhs = restrict(fine_res)
    middle_sol, middle_res = descend(middle_rhs, 1)
    third_rhs = restrict(middle_res)
    third_sol, third_res = descend(third_rhs, 2)
    coarse_sol = coarsest(restrict(third_res))
    third_sol = ascend(third_sol + prolong(coarse_sol), third_rhs, 2)
    middle_sol = ascend(middle_sol + prolong(third_sol), middle_rhs, 1)
    velocity = ascend(fine_sol + prolong(middle_sol), source, 0)
    velocity_low = velocity.astype(jnp.bfloat16)

    def pick(group_target, group_base):
        return velocity_low[box_index(group_target, group_base)].reshape(group_target.shape[0], -1)

    picked = grouped(pick, (target, base_cells), group_rows)
    marker_velocity = grouped(read_boxes, (marker_positions, picked), group_rows)
    return velocity, marker_velocity
```

```python
import jax
import jax.numpy as jnp
from jax import lax
from jax.experimental import pallas as pl
from jax.experimental.pallas import tpu as pltpu
from jax.sharding import PartitionSpec as P

CZ = 4
BOX = 16
SWEEPS = 2
CSWEEPS = 6


screening = 1.0 / 64.0
relaxation = 2.0 / 3.0


def padded_2(array, sides, width):
    for axis, dim in sides:
        size, length = (lax.axis_size(axis), array.shape[dim])
        up = [(i, (i + 1) % size) for i in range(size)]
        down = [(j, i) for i, j in up]
        last = lax.slice_in_dim(array, length - width, length, axis=dim)
        initial = lax.slice_in_dim(array, 0, width, axis=dim)
        before = lax.ppermute(last, axis, up)
        after = lax.ppermute(initial, axis, down)
        array = jnp.concatenate([before, array, after], axis=dim)
    return array


ROWS = 2 * CZ * 3
HALF = CZ * 3
PACK = 8


def marker_tables(positions):
    scale = jnp.array([BOX - 5.0, BOX - 5.0, CZ - 1.0], jnp.float32)[None, :, None]
    shift = jnp.array([2.0, 2.0, 0.0], jnp.float32)[None, :, None]
    place = shift + scale * positions
    turn = 0.5 * jnp.pi * (place - 4.0 * jnp.floor(0.25 * place))
    return jnp.concatenate([place, jnp.cos(turn), jnp.sin(turn)], axis=1)


def phi_rows(table, axis, cell):
    quarter = cell & 3
    along_cos = jnp.where(quarter == 0, 1.0, jnp.where(quarter == 2, -1.0, 0.0))
    along_sin = jnp.where(quarter == 1, 1.0, jnp.where(quarter == 3, -1.0, 0.0))
    offset = table[axis : axis + 1] - cell.astype(jnp.float32)
    wave = along_cos * table[3 + axis : 4 + axis] + along_sin * table[6 + axis : 7 + axis]
    return jnp.where(jnp.abs(offset) < 2.0, 0.25 + 0.25 * wave, 0.0)


def split_two(value):
    high = value.astype(jnp.bfloat16)
    return high, (value - high.astype(jnp.float32)).astype(jnp.bfloat16)


def block_weights(table):
    marks = table.shape[1]
    cell = lax.broadcasted_iota(jnp.int32, (BOX, marks), 0)
    weight_x = phi_rows(table, 0, cell)
    weight_y = phi_rows(table, 1, cell)
    weight_z = phi_rows(table, 2, cell & (CZ - 1))
    plane = (weight_x[:, None, :] * weight_y[None, :, :]).reshape(BOX * BOX, marks)
    return weight_z, split_two(plane)


def build_kernel(slot_ref, table_ref, force_ref, out_ref, box_ref):
    blocks, marks = table_ref.shape[0], table_ref.shape[2]
    box_ref[...] = jnp.zeros_like(box_ref)

    def one(block):
        weight_z, (plane_high, plane_low) = block_weights(table_ref[block])
        force = force_ref[block]
        row = lax.broadcasted_iota(jnp.int32, (BOX, marks), 0)
        force = jnp.where(
            row < CZ,
            force[0:1],
            jnp.where(row < 2 * CZ, force[1:2], jnp.where(row < 3 * CZ, force[2:3], 0.0)),
        )
        loaded = jnp.concatenate(split_two(weight_z * force), axis=0)
        dims = (((1,), (1,)), ((), ()))
        both = lax.dot_general(loaded, plane_high, dims, preferred_element_type=jnp.float32)
        both = both + lax.dot_general(loaded, plane_low, dims, preferred_element_type=jnp.float32)
        box = both[:BOX] + both[BOX:]
        slot = slot_ref[block]
        box_ref[slot, 0:HALF, :] = box[:HALF, :128]
        box_ref[slot, HALF:ROWS, :] = box[:HALF, 128:]

    def some(turn, carry):
        for part in range(4):
            one(turn * 4 + part)
        return carry

    lax.fori_loop(0, blocks // 4, some, 0)
    pack_boxes(box_ref, out_ref)


def pack_boxes(box_ref, out_ref):
    def pack(turn, carry):
        boxes = box_ref[pl.ds(turn * PACK, PACK)]
        out_ref[pl.ds(pl.multiple_of(turn * PACK * ROWS, PACK * ROWS), PACK * ROWS), :] = (
            boxes.reshape(PACK * ROWS, 128).astype(jnp.bfloat16)
        )
        return carry

    lax.fori_loop(0, box_ref.shape[0] // PACK, pack, 0)


def unpack_boxes(in_ref, box_ref):
    def unpack(turn, carry):
        rows = in_ref[pl.ds(pl.multiple_of(turn * PACK * ROWS, PACK * ROWS), PACK * ROWS), :]
        box_ref[pl.ds(turn * PACK, PACK)] = rows.astype(jnp.float32).reshape(PACK, ROWS, 128)
        return carry

    lax.fori_loop(0, box_ref.shape[0] // PACK, unpack, 0)


def read_kernel(slot_ref, table_ref, in_ref, out_ref, box_ref):
    blocks = table_ref.shape[0]
    unpack_boxes(in_ref, box_ref)

    def one(block):
        weight_z, (plane_high, plane_low) = block_weights(table_ref[block])
        slot = slot_ref[block]
        first = box_ref[slot, 0:BOX, :]
        second = box_ref[slot, HALF - 4 : ROWS, :]
        second = pltpu.roll(second, BOX - 4, 0)
        box = jnp.concatenate([first, second], axis=1).astype(jnp.bfloat16)
        spread = jnp.dot(box, plane_high, preferred_element_type=jnp.float32)
        spread = spread + jnp.dot(box, plane_low, preferred_element_type=jnp.float32)
        spread = spread * weight_z
        for component in range(3):
            out_ref[block, component : component + 1, :] = jnp.sum(
                spread[component * CZ : (component + 1) * CZ], axis=0, keepdims=True
            )

    def some(turn, carry):
        for part in range(4):
            one(turn * 4 + part)
        return carry

    lax.fori_loop(0, blocks // 4, some, 0)


def place_kernel(base_ref, in_ref, fluid_ref, out_ref, box_ref, grid_ref):
    slots, width = box_ref.shape[0], fluid_ref.shape[2]
    unpack_boxes(in_ref, box_ref)
    grid_ref[...] = jnp.zeros_like(grid_ref)
    lane = lax.broadcasted_iota(jnp.int32, (ROWS, 128), 1)

    def one(slot):
        first_x, first_y = base_ref[2 * slot], base_ref[2 * slot + 1]

        @pl.when(first_x >= 0)
        def _():
            box = box_ref[slot]
            inside = ((lane - first_y) & (width - 1)) < BOX
            for step in range(8):
                moved = pltpu.roll(box, (first_y - BOX * step) & (width - 1), 1)
                x = (first_x + step) & (width - 1)
                grid_ref[x] += jnp.where(inside, moved, 0.0)

    def some(turn, carry):
        for part in range(4):
            one(turn * 4 + part)
        return carry

    lax.fori_loop(0, slots // 4, some, 0)
    for layer in range(CZ):
        for component in range(3):
            row = component * CZ + layer
            near = grid_ref[:, row, :]
            far = pltpu.roll(grid_ref[:, HALF + row, :], 8, 0)
            out_ref[layer, component] = fluid_ref[layer, component] + (near + far)


def pick_kernel(base_ref, velocity_ref, out_ref, box_ref, grid_ref):
    slots, width = box_ref.shape[0], velocity_ref.shape[2]
    for layer in range(CZ):
        for component in range(3):
            row = component * CZ + layer
            low = velocity_ref[layer, component].astype(jnp.bfloat16).astype(jnp.float32)
            grid_ref[:, row, :] = low
            grid_ref[:, HALF + row, :] = pltpu.roll(low, width - 8, 0)
    lane = lax.broadcasted_iota(jnp.int32, (ROWS, 128), 1)

    def one(slot):
        first_x, first_y = base_ref[2 * slot], base_ref[2 * slot + 1]

        @pl.when(first_x < 0)
        def _():
            box_ref[slot] = jnp.zeros((ROWS, 128), jnp.float32)

        @pl.when(first_x >= 0)
        def _():
            box = jnp.zeros((ROWS, 128), jnp.float32)
            for step in range(8):
                x = (first_x + step) & (width - 1)
                moved = pltpu.roll(grid_ref[x], (BOX * step - first_y) & (width - 1), 1)
                box = jnp.where(lane // BOX == step, moved, box)
            box_ref[slot] = box

    def some(turn, carry):
        for part in range(4):
            one(turn * 4 + part)
        return carry

    lax.fori_loop(0, slots // 4, some, 0)
    pack_boxes(box_ref, out_ref)


VM = pl.BlockSpec(memory_space=pltpu.VMEM)
SM = pl.BlockSpec(memory_space=pltpu.SMEM)


def local_call(body, out, specs, scratch, name):
    return pl.pallas_call(
        body,
        out_shape=out,
        in_specs=specs,
        out_specs=VM,
        scratch_shapes=scratch,
        name=name,
        compiler_params=pltpu.CompilerParams(vmem_limit_bytes=56 * 2**20),
    )


def operate(solution, level_index, shared):
    if shared:
        padded = padded_2(solution, (("gz", 0),), 1)
        upper_layer = padded[2:]
        lower_layer = padded[:-2]
    else:
        upper_layer = jnp.roll(solution, -1, 0)
        lower_layer = jnp.roll(solution, 1, 0)
    beside = upper_layer + lower_layer
    beside = beside + jnp.roll(solution, -1, 2) + jnp.roll(solution, 1, 2)
    beside = beside + jnp.roll(solution, -1, 3) + jnp.roll(solution, 1, 3)
    return screening * solution - 0.25**level_index * (beside - 6.0 * solution)


def relax_factor(level_index):
    return relaxation / (screening + 6.0 * 0.25**level_index)


def halver(width):
    cells = jnp.arange(width) // 2
    return (cells[:, None] == jnp.arange(width // 2)[None, :]).astype(jnp.float32)


def restrict(solution):
    pairs = solution[0::2] + solution[1::2]
    half = halver(solution.shape[3])
    pairs = jnp.einsum("zcxy,yY->zcxY", pairs, half, precision=lax.Precision.HIGHEST)
    return 0.125 * jnp.einsum("zcxY,xX->zcXY", pairs, half, precision=lax.Precision.HIGHEST)


def prolong(solution):
    half = halver(2 * solution.shape[3])
    wide = jnp.einsum("zcXY,yY->zcXy", solution, half, precision=lax.Precision.HIGHEST)
    wide = jnp.einsum("zcXy,xX->zcxy", wide, half, precision=lax.Precision.HIGHEST)
    return jnp.repeat(wide, 2, 0)


def descend(source, level_index, shared):
    factor = relax_factor(level_index)
    solution = factor * source
    solution = solution + factor * (source - operate(solution, level_index, shared))
    return (solution, source - operate(solution, level_index, shared))


def ascend(solution, source, level_index, shared):
    factor = relax_factor(level_index)
    for sweep_turn in range(SWEEPS):
        solution = solution + factor * (source - operate(solution, level_index, shared))
    return solution


def coarsest(source):
    factor = relax_factor(3)
    solution = factor * source
    for sweep_turn in range(CSWEEPS - 1):
        solution = solution + factor * (source - operate(solution, 3, False))
    leftover = source - operate(solution, 3, False)
    level_mean = jnp.mean(leftover, axis=(0, 2, 3), keepdims=True)
    return solution + level_mean / screening


def collect(layers_here):
    return lax.all_gather(layers_here, "gz", axis=0, tiled=True)


def shards(marker_positions, marker_forces, dest_slab, base_cells, fluid_source):
    devices = lax.axis_size("gz")
    held_blocks = marker_positions.shape[0]
    width = fluid_source.shape[2]
    capacity = max(2, 2 * held_blocks // devices)
    slots = devices * capacity
    target = dest_slab[:, 0]
    dest_hits = (target[:, None] == jnp.arange(devices, dtype=jnp.int32)[None, :]).astype(jnp.int32)
    earlier = jnp.arange(held_blocks)[:, None] > jnp.arange(held_blocks)[None, :]
    slot_order = jnp.sum((earlier & (target[:, None] == target[None, :])).astype(jnp.int32), axis=1)
    slot_index = target * capacity + slot_order
    slot_hits = slot_index[None, :] == jnp.arange(slots, dtype=jnp.int32)[:, None]
    base_sent = jnp.sum(
        jnp.where(slot_hits[:, :, None], base_cells[None, :, :] + 1, 0), axis=1
    )
    arrived_base = lax.all_to_all(
        base_sent.reshape(devices, capacity * 2), "gz", split_axis=0, concat_axis=0, tiled=True
    )
    arrived_base = arrived_base.reshape(-1) - 1
    tables = marker_tables(marker_positions)
    boxes = pltpu.VMEM((slots, ROWS, 128), jnp.float32)
    grid = pltpu.VMEM((width, ROWS, 128), jnp.float32)
    packed = jax.ShapeDtypeStruct((slots * ROWS, 128), jnp.bfloat16)
    box_sent = local_call(build_kernel, packed, [SM, VM, VM], [boxes], "build")(
        slot_index, tables, marker_forces
    )
    arrived = lax.all_to_all(box_sent, "gz", split_axis=0, concat_axis=0, tiled=True)
    source = local_call(
        place_kernel,
        jax.ShapeDtypeStruct(fluid_source.shape, jnp.float32),
        [SM, VM, VM],
        [boxes, grid],
        "place",
    )(arrived_base, arrived, fluid_source)
    velocity = multigrid(source)
    picked = local_call(pick_kernel, packed, [SM, VM], [boxes, grid], "pick")(
        arrived_base, velocity
    )
    returned = lax.all_to_all(picked, "gz", split_axis=0, concat_axis=0, tiled=True)
    marker_velocity = local_call(
        read_kernel,
        jax.ShapeDtypeStruct(marker_positions.shape, jnp.float32),
        [SM, VM, VM],
        [boxes],
        "read",
    )(slot_index, tables, returned)
    return (velocity, marker_velocity)


def multigrid(source):
    fine_sol, fine_res = descend(source, 0, True)
    middle_rhs = restrict(fine_res)
    middle_sol, middle_res = descend(middle_rhs, 1, True)
    third_rhs = restrict(middle_res)
    layers = third_rhs.shape[0]
    first_layer = lax.axis_index("gz") * layers
    whole_rhs = collect(third_rhs)
    whole_sol, whole_res = descend(whole_rhs, 2, False)
    coarse_sol = coarsest(restrict(whole_res))
    whole_sol = ascend(whole_sol + prolong(coarse_sol), whole_rhs, 2, False)
    third_sol = lax.dynamic_slice_in_dim(whole_sol, first_layer, layers, 0)
    middle_sol = ascend(middle_sol + prolong(third_sol), middle_rhs, 1, True)
    velocity = ascend(fine_sol + prolong(middle_sol), source, 0, True)
    return velocity


def solution(mesh):
    placed = (
        P("gz", None, None),
        P("gz", None, None),
        P("gz", None),
        P("gz", None),
        P("gz", None, None, None),
    )
    return jax.shard_map(
        shards,
        mesh=mesh,
        in_specs=placed,
        out_specs=(P("gz", None, None, None), P("gz", None, None)),
        check_vma=False,
    )
```

```python
import functools

import jax
import jax.numpy as jnp
from jax import lax
from jax.experimental import pallas as pl
from jax.experimental.pallas import tpu as pltpu
from jax.sharding import PartitionSpec as P

CZ = 4
BOX = 16
SWEEPS = 2
CSWEEPS = 6


screening = 1.0 / 64.0
relaxation = 2.0 / 3.0


def padded_2(array, sides, width):
    for axis, dim in sides:
        size, length = (lax.axis_size(axis), array.shape[dim])
        up = [(i, (i + 1) % size) for i in range(size)]
        down = [(j, i) for i, j in up]
        last = lax.slice_in_dim(array, length - width, length, axis=dim)
        initial = lax.slice_in_dim(array, 0, width, axis=dim)
        before = lax.ppermute(last, axis, up)
        after = lax.ppermute(initial, axis, down)
        array = jnp.concatenate([before, array, after], axis=dim)
    return array


ROWS = 2 * CZ * 3
HALF = CZ * 3
PACK = 8


def marker_tables(positions):
    scale = jnp.array([BOX - 5.0, BOX - 5.0, CZ - 1.0], jnp.float32)[None, :, None]
    shift = jnp.array([2.0, 2.0, 0.0], jnp.float32)[None, :, None]
    place = shift + scale * positions
    turn = 0.5 * jnp.pi * (place - 4.0 * jnp.floor(0.25 * place))
    return jnp.concatenate([place, jnp.cos(turn), jnp.sin(turn)], axis=1)


def phi_rows(table, axis, cell):
    quarter = cell & 3
    along_cos = jnp.where(quarter == 0, 1.0, jnp.where(quarter == 2, -1.0, 0.0))
    along_sin = jnp.where(quarter == 1, 1.0, jnp.where(quarter == 3, -1.0, 0.0))
    offset = table[axis : axis + 1] - cell.astype(jnp.float32)
    wave = along_cos * table[3 + axis : 4 + axis] + along_sin * table[6 + axis : 7 + axis]
    return jnp.where(jnp.abs(offset) < 2.0, 0.25 + 0.25 * wave, 0.0)


def split_two(value):
    high = value.astype(jnp.bfloat16)
    return high, (value - high.astype(jnp.float32)).astype(jnp.bfloat16)


def block_weights(table):
    marks = table.shape[1]
    cell = lax.broadcasted_iota(jnp.int32, (BOX, marks), 0)
    weight_x = phi_rows(table, 0, cell)
    weight_y = phi_rows(table, 1, cell)
    weight_z = phi_rows(table, 2, cell & (CZ - 1))
    plane = (weight_x[:, None, :] * weight_y[None, :, :]).reshape(BOX * BOX, marks)
    return weight_z, split_two(plane)


def build_kernel(slot_ref, table_ref, force_ref, out_ref, box_ref):
    blocks, marks = table_ref.shape[0], table_ref.shape[2]
    box_ref[...] = jnp.zeros_like(box_ref)

    def one(block):
        weight_z, (plane_high, plane_low) = block_weights(table_ref[block])
        force = force_ref[block]
        row = lax.broadcasted_iota(jnp.int32, (BOX, marks), 0)
        force = jnp.where(
            row < CZ,
            force[0:1],
            jnp.where(row < 2 * CZ, force[1:2], jnp.where(row < 3 * CZ, force[2:3], 0.0)),
        )
        loaded = jnp.concatenate(split_two(weight_z * force), axis=0)
        dims = (((1,), (1,)), ((), ()))
        both = lax.dot_general(loaded, plane_high, dims, preferred_element_type=jnp.float32)
        both = both + lax.dot_general(loaded, plane_low, dims, preferred_element_type=jnp.float32)
        box = both[:BOX] + both[BOX:]
        slot = slot_ref[block]
        box_ref[slot, 0:HALF, :] = box[:HALF, :128]
        box_ref[slot, HALF:ROWS, :] = box[:HALF, 128:]

    def some(turn, carry):
        for part in range(4):
            one(turn * 4 + part)
        return carry

    lax.fori_loop(0, blocks // 4, some, 0)
    pack_boxes(box_ref, out_ref)


def pack_boxes(box_ref, out_ref):
    def pack(turn, carry):
        boxes = box_ref[pl.ds(turn * PACK, PACK)]
        out_ref[pl.ds(pl.multiple_of(turn * PACK * ROWS, PACK * ROWS), PACK * ROWS), :] = (
            boxes.reshape(PACK * ROWS, 128).astype(jnp.bfloat16)
        )
        return carry

    lax.fori_loop(0, box_ref.shape[0] // PACK, pack, 0)


def unpack_boxes(in_ref, box_ref):
    def unpack(turn, carry):
        rows = in_ref[pl.ds(pl.multiple_of(turn * PACK * ROWS, PACK * ROWS), PACK * ROWS), :]
        box_ref[pl.ds(turn * PACK, PACK)] = rows.astype(jnp.float32).reshape(PACK, ROWS, 128)
        return carry

    lax.fori_loop(0, box_ref.shape[0] // PACK, unpack, 0)


def read_kernel(slot_ref, table_ref, in_ref, out_ref, box_ref):
    blocks = table_ref.shape[0]
    unpack_boxes(in_ref, box_ref)

    def one(block):
        weight_z, (plane_high, plane_low) = block_weights(table_ref[block])
        slot = slot_ref[block]
        first = box_ref[slot, 0:BOX, :]
        second = box_ref[slot, HALF - 4 : ROWS, :]
        second = pltpu.roll(second, BOX - 4, 0)
        box = jnp.concatenate([first, second], axis=1).astype(jnp.bfloat16)
        spread = jnp.dot(box, plane_high, preferred_element_type=jnp.float32)
        spread = spread + jnp.dot(box, plane_low, preferred_element_type=jnp.float32)
        spread = spread * weight_z
        for component in range(3):
            out_ref[block, component : component + 1, :] = jnp.sum(
                spread[component * CZ : (component + 1) * CZ], axis=0, keepdims=True
            )

    def some(turn, carry):
        for part in range(4):
            one(turn * 4 + part)
        return carry

    lax.fori_loop(0, blocks // 4, some, 0)


def place_kernel(base_ref, in_ref, fluid_ref, out_ref, box_ref, grid_ref):
    slots, width = box_ref.shape[0], fluid_ref.shape[2]
    unpack_boxes(in_ref, box_ref)
    grid_ref[...] = jnp.zeros_like(grid_ref)
    lane = lax.broadcasted_iota(jnp.int32, (ROWS, 128), 1)

    def one(slot):
        first_x, first_y = base_ref[2 * slot], base_ref[2 * slot + 1]

        @pl.when(first_x >= 0)
        def _():
            box = box_ref[slot]
            inside = ((lane - first_y) & (width - 1)) < BOX
            for step in range(8):
                moved = pltpu.roll(box, (first_y - BOX * step) & (width - 1), 1)
                x = (first_x + step) & (width - 1)
                grid_ref[x] += jnp.where(inside, moved, 0.0)

    def some(turn, carry):
        for part in range(4):
            one(turn * 4 + part)
        return carry

    lax.fori_loop(0, slots // 4, some, 0)
    for layer in range(CZ):
        for component in range(3):
            row = component * CZ + layer
            near = grid_ref[:, row, :]
            far = pltpu.roll(grid_ref[:, HALF + row, :], 8, 0)
            out_ref[layer, component] = fluid_ref[layer, component] + (near + far)


def pick_kernel(base_ref, velocity_ref, out_ref, box_ref, grid_ref):
    slots, width = box_ref.shape[0], velocity_ref.shape[2]
    for layer in range(CZ):
        for component in range(3):
            row = component * CZ + layer
            low = velocity_ref[layer, component].astype(jnp.bfloat16).astype(jnp.float32)
            grid_ref[:, row, :] = low
            grid_ref[:, HALF + row, :] = pltpu.roll(low, width - 8, 0)
    lane = lax.broadcasted_iota(jnp.int32, (ROWS, 128), 1)

    def one(slot):
        first_x, first_y = base_ref[2 * slot], base_ref[2 * slot + 1]

        @pl.when(first_x < 0)
        def _():
            box_ref[slot] = jnp.zeros((ROWS, 128), jnp.float32)

        @pl.when(first_x >= 0)
        def _():
            box = jnp.zeros((ROWS, 128), jnp.float32)
            for step in range(8):
                x = (first_x + step) & (width - 1)
                moved = pltpu.roll(grid_ref[x], (BOX * step - first_y) & (width - 1), 1)
                box = jnp.where(lane // BOX == step, moved, box)
            box_ref[slot] = box

    def some(turn, carry):
        for part in range(4):
            one(turn * 4 + part)
        return carry

    lax.fori_loop(0, slots // 4, some, 0)
    pack_boxes(box_ref, out_ref)


VM = pl.BlockSpec(memory_space=pltpu.VMEM)
SM = pl.BlockSpec(memory_space=pltpu.SMEM)


def local_call(body, out, specs, scratch, name):
    return pl.pallas_call(
        body,
        out_shape=out,
        in_specs=specs,
        out_specs=VM,
        scratch_shapes=scratch,
        name=name,
        compiler_params=pltpu.CompilerParams(vmem_limit_bytes=56 * 2**20),
    )


def factor_of(level):
    return relaxation / (screening + 6.0 * 0.25**level)


def wide_dot(left, right):
    return jnp.dot(
        left, right, precision=lax.Precision.HIGHEST, preferred_element_type=jnp.float32
    )


def table(rows, columns, rule):
    row = lax.broadcasted_iota(jnp.int32, (rows, columns), 0)
    column = lax.broadcasted_iota(jnp.int32, (rows, columns), 1)
    return jnp.where(rule(row, column), 1.0, 0.0).astype(jnp.float32)


def beside(value, group_rows, group):
    axis = value.ndim - 2
    rows, lanes = value.shape[axis], value.shape[axis + 1]
    right = pltpu.roll(value, lanes - 1, axis + 1)
    left = pltpu.roll(value, 1, axis + 1)
    after = pltpu.roll(value, rows - 1, axis)
    before = pltpu.roll(value, 1, axis)
    if group < lanes:
        lane = lax.broadcasted_iota(jnp.int32, value.shape, axis + 1) & (group - 1)
        row = lax.broadcasted_iota(jnp.int32, value.shape, axis) & (group_rows - 1)
        right = jnp.where(lane == group - 1, pltpu.roll(value, group - 1, axis + 1), right)
        left = jnp.where(lane == 0, pltpu.roll(value, lanes - group + 1, axis + 1), left)
        wrap_after, wrap_before = after, before
        if group_rows < rows:
            wrap_after = pltpu.roll(value, group_rows - 1, axis)
            wrap_before = pltpu.roll(value, rows - group_rows + 1, axis)
        after = jnp.where(
            row == group_rows - 1, pltpu.roll(wrap_after, lanes - group, axis + 1), after
        )
        before = jnp.where(row == 0, pltpu.roll(wrap_before, group, axis + 1), before)
    return (right + left) + (after + before)


def first_sweep(source, around, level):
    factor = factor_of(level)
    return (4.0 / 3.0 * factor) * source + (factor * factor * 0.25**level) * around


def next_sweep(solution, source, around, level):
    factor = factor_of(level)
    return (1.0 - relaxation) * solution + factor * source + (factor * 0.25**level) * around


def left_over(solution, source, around, level):
    return source - (screening + 6.0 * 0.25**level) * solution + 0.25**level * around


def grid_kernel(
    devices,
    source_ref,
    out_ref,
    b0,
    u0,
    t0,
    b1,
    u1,
    t1,
    f1,
    b2,
    u2,
    send0,
    recv0,
    send1,
    recv1,
    send2,
    recv2,
):
    me = lax.axis_index("gz")

    def other(step):
        return lax.rem(me + step + devices, devices)

    barrier = pltpu.get_barrier_semaphore()

    def greet(step, carry):
        pl.semaphore_signal(
            barrier, inc=1, device_id=(other(step),), device_id_type=pl.DeviceIdType.MESH
        )
        return carry

    lax.fori_loop(1, devices, greet, 0)
    pl.semaphore_wait(barrier, devices - 1)

    def send(src, dst, send_sem, recv_sem, step):
        copy = pltpu.make_async_remote_copy(
            src_ref=src,
            dst_ref=dst,
            send_sem=send_sem,
            recv_sem=recv_sem,
            device_id=(other(step),),
            device_id_type=pl.DeviceIdType.MESH,
        )
        copy.start()
        return copy

    width, lanes = source_ref.shape[2], source_ref.shape[3]
    near = [
        send(source_ref.at[2:4], b0.at[1:3], send0.at[0], recv0.at[0], 1),
        send(source_ref.at[0:2], b0.at[7:9], send0.at[1], recv0.at[1], -1),
    ]
    far = [
        send(source_ref.at[1:2], b0.at[0:1], send0.at[2], recv0.at[2], 1),
        send(source_ref.at[2:3], b0.at[9:10], send0.at[3], recv0.at[3], -1),
    ]

    def loop(low, high, body):
        def step(turn, carry):
            for component in range(3):
                body(turn, component)
            return carry

        lax.fori_loop(low, high, step, 0)

    def keep(z, c):
        b0[z + 3, c] = source_ref[z, c]

    loop(0, 4, keep)

    def begin0(z, c):
        here = b0[z, c]
        around = beside(here, width, lanes) + (b0[z - 1, c] + b0[z + 1, c])
        u0[z - 1, c] = first_sweep(here, around, 0)

    loop(4, 6, begin0)
    for copy in near:
        copy.wait()
    loop(2, 4, begin0)
    loop(6, 8, begin0)

    half = width // 2
    fold0 = table(half, width, lambda r, c: c // 2 == r)
    pack0 = [
        table(lanes, lanes, lambda r, c, a=a: (c // half == a) & (r // 2 == c % half))
        for a in range(2)
    ]
    quarter = half // 2
    fold1 = table(quarter // 2, quarter, lambda r, c: c // 2 == r)
    rows1, rows2 = quarter, quarter // 4
    group1, group2 = half, quarter

    def rest0(z, c):
        here = u0[z + 2, c]
        around = beside(here, width, lanes) + (u0[z + 1, c] + u0[z + 3, c])
        return left_over(here, b0[z + 3, c], around, 0)

    def down0(z1, c):
        pair = 0.125 * (rest0(2 * z1, c) + rest0(2 * z1 + 1, c))
        folded = wide_dot(fold0, pair)
        b1[z1 + 4, c] = wide_dot(folded[:rows1], pack0[0]) + wide_dot(folded[rows1:], pack0[1])

    loop(0, 2, down0)
    near1 = [
        send(b1.at[4:6], b1.at[2:4], send1.at[0], recv1.at[0], 1),
        send(b1.at[4:6], b1.at[6:8], send1.at[1], recv1.at[1], -1),
    ]
    far1 = [
        send(b1.at[4:6], b1.at[0:2], send1.at[2], recv1.at[2], 2),
        send(b1.at[4:6], b1.at[8:10], send1.at[3], recv1.at[3], -2),
    ]

    def begin1(z, c):
        here = b1[z, c]
        around = beside(here, rows1, group1) + (b1[z - 1, c] + b1[z + 1, c])
        u1[z - 1, c] = first_sweep(here, around, 1)

    for copy in near1:
        copy.wait()
    loop(3, 7, begin1)

    def rest1(z, c):
        here = u1[z + 3, c]
        around = beside(here, rows1, group1) + (u1[z + 2, c] + u1[z + 4, c])
        return left_over(here, b1[z + 4, c], around, 1)

    pack1 = [
        table(
            lanes,
            lanes,
            lambda r, c, a=a: (c // group2 == 2 * (r // group1) + a)
            & (c % group2 == (r % group1) // 2),
        )
        for a in range(2)
    ]
    for c in range(3):
        folded = wide_dot(fold1, 0.125 * (rest1(0, c) + rest1(1, c)))
        b2[me, c] = wide_dot(folded[:rows2], pack1[0]) + wide_dot(folded[rows2:], pack1[1])

    def spread(step, carry):
        send(b2.at[me], b2.at[me], send2, recv2, step)
        return carry

    lax.fori_loop(1, devices, spread, 0)
    for copy in far:
        copy.wait()
    loop(1, 2, begin0)
    loop(8, 9, begin0)
    for copy in far1:
        copy.wait()
    loop(1, 3, begin1)
    loop(7, 9, begin1)
    rest = b2.at[0 : devices - 1]
    pltpu.make_async_copy(rest, rest, send2).wait()
    pltpu.make_async_copy(rest, rest, recv2).wait()

    count = 3 * devices
    half2 = devices // 2
    group3 = group2 // 2
    rhs2 = b2[...].reshape(count, rows2, lanes)

    def around2(value):
        ends = jnp.concatenate([value[3:], value[:3]], 0) + jnp.concatenate(
            [value[-3:], value[:-3]], 0
        )
        return beside(value, rows2, group2) + ends

    sol2 = first_sweep(rhs2, around2(rhs2), 2)
    left2 = left_over(sol2, rhs2, around2(sol2), 2).reshape(half2, 2, 3 * rows2, lanes)
    left2 = (0.125 * (left2[:, 0] + left2[:, 1])).reshape(half2 * 3 * rows2, lanes)
    span3 = 4 * group3
    pack2 = table(
        lanes,
        lanes,
        lambda r, c: ((c % span3) // group3 == r // group2) & (c % group3 == (r % group2) // 2),
    )
    rows3 = rows2 // 2
    fold2 = table(
        4 * rows3,
        3 * rows2,
        lambda r, c: (c // rows2 == r // rows3) & ((c % rows2) // 2 == r % rows3),
    )
    left2 = wide_dot(left2, pack2).reshape(half2, 3 * rows2, lanes)
    rhs3 = jnp.stack([wide_dot(fold2, left2[z]) for z in range(half2)], 0)

    def around3(value):
        ends = jnp.concatenate([value[1:], value[:1]], 0) + jnp.concatenate(
            [value[-1:], value[:-1]], 0
        )
        return beside(value, rows3, group3) + ends

    sol3 = first_sweep(rhs3, around3(rhs3), 3)
    for turn in range(CSWEEPS - 2):
        sol3 = next_sweep(sol3, rhs3, around3(sol3), 3)
    total = jnp.sum(left_over(sol3, rhs3, around3(sol3), 3), axis=0)
    total = jnp.broadcast_to(jnp.sum(total, axis=1, keepdims=True), total.shape)
    same = table(4 * rows3, 4 * rows3, lambda r, c: r // rows3 == c // rows3)
    cells = half2 * rows3 * lanes
    sol3 = sol3 + (wide_dot(same, total) * (1.0 / (screening * cells)))[None]

    open2 = table(
        lanes,
        lanes,
        lambda r, c: (r < span3)
        & (r // group3 == c // group2)
        & (r % group3 == (c % group2) // 2),
    )
    rise2 = table(
        3 * rows2,
        4 * rows3,
        lambda r, c: (r // rows2 == c // rows3) & ((r % rows2) // 2 == c % rows3),
    )
    lift = jnp.concatenate([wide_dot(rise2, sol3[z]) for z in range(half2)], 0)
    lift = wide_dot(lift, open2).reshape(half2, 1, 3 * rows2, lanes)
    lift = jnp.concatenate([lift, lift], axis=1).reshape(count, rows2, lanes)
    sol2 = sol2 + lift
    for turn in range(SWEEPS):
        sol2 = next_sweep(sol2, rhs2, around2(sol2), 2)
    u2[...] = sol2.reshape(devices, 3, rows2, lanes)

    rise1 = table(quarter, quarter // 2, lambda r, c: r // 2 == c)
    open1 = [
        table(
            lanes,
            lanes,
            lambda r, c, a=a: (r // group2 == 2 * (c // group1) + a)
            & (r % group2 == (c % group1) // 2),
        )
        for a in range(2)
    ]

    def lift1(z2, c):
        coarse = u2[other(z2 - 2), c]
        tall = jnp.concatenate([wide_dot(coarse, open1[0]), wide_dot(coarse, open1[1])], 0)
        return wide_dot(rise1, tall)

    for c in range(3):
        u1[0, c] += lift1(0, c)
        u1[7, c] += lift1(4, c)

    def raise1(z2, c):
        up = lift1(z2, c)
        u1[2 * z2 - 1, c] += up
        u1[2 * z2, c] += up

    loop(1, 4, raise1)

    def later1(z, c):
        here = u1[z, c]
        around = beside(here, rows1, group1) + (u1[z - 1, c] + u1[z + 1, c])
        t1[z - 1, c] = next_sweep(here, b1[z + 1, c], around, 1)

    loop(1, 7, later1)

    def last1(z, c):
        here = t1[z, c]
        around = beside(here, rows1, group1) + (t1[z - 1, c] + t1[z + 1, c])
        f1[z - 1, c] = next_sweep(here, b1[z + 2, c], around, 1)

    loop(1, 5, last1)

    rise0 = table(width, half, lambda r, c: r // 2 == c)
    open0 = [
        table(lanes, lanes, lambda r, c, a=a: (r // half == a) & (c // 2 == r % half))
        for a in range(2)
    ]

    def raise0(z1, c):
        coarse = f1[z1, c]
        tall = jnp.concatenate([wide_dot(coarse, open0[0]), wide_dot(coarse, open0[1])], 0)
        up = wide_dot(rise0, tall)
        u0[2 * z1, c] += up
        u0[2 * z1 + 1, c] += up

    loop(0, 4, raise0)

    def later0(z, c):
        here = u0[z, c]
        around = beside(here, width, lanes) + (u0[z - 1, c] + u0[z + 1, c])
        t0[z - 1, c] = next_sweep(here, b0[z + 1, c], around, 0)

    loop(1, 7, later0)

    def last0(z, c):
        here = t0[z, c]
        around = beside(here, width, lanes) + (t0[z - 1, c] + t0[z + 1, c])
        out_ref[z - 1, c] = next_sweep(here, b0[z + 2, c], around, 0)

    loop(1, 5, last0)


def multigrid(source):
    devices = lax.axis_size("gz")
    width = source.shape[3]
    fine, middle, third = (3, width, width), (3, width // 4, width), (3, width // 16, width)
    dma = pltpu.SemaphoreType.DMA
    scratch = [
        pltpu.VMEM((10,) + fine, jnp.float32),
        pltpu.VMEM((8,) + fine, jnp.float32),
        pltpu.VMEM((6,) + fine, jnp.float32),
        pltpu.VMEM((10,) + middle, jnp.float32),
        pltpu.VMEM((8,) + middle, jnp.float32),
        pltpu.VMEM((6,) + middle, jnp.float32),
        pltpu.VMEM((4,) + middle, jnp.float32),
        pltpu.VMEM((devices,) + third, jnp.float32),
        pltpu.VMEM((devices,) + third, jnp.float32),
        dma((4,)),
        dma((4,)),
        dma((4,)),
        dma((4,)),
        dma,
        dma,
    ]
    return pl.pallas_call(
        functools.partial(grid_kernel, devices),
        out_shape=jax.ShapeDtypeStruct(source.shape, jnp.float32),
        in_specs=[VM],
        out_specs=VM,
        scratch_shapes=scratch,
        name="multigrid",
        compiler_params=pltpu.CompilerParams(
            collective_id=0, has_side_effects=True, vmem_limit_bytes=56 * 2**20
        ),
    )(source)


def shards(marker_positions, marker_forces, dest_slab, base_cells, fluid_source):
    devices = lax.axis_size("gz")
    held_blocks = marker_positions.shape[0]
    width = fluid_source.shape[2]
    capacity = max(2, 2 * held_blocks // devices)
    slots = devices * capacity
    target = dest_slab[:, 0]
    dest_hits = (target[:, None] == jnp.arange(devices, dtype=jnp.int32)[None, :]).astype(jnp.int32)
    earlier = jnp.arange(held_blocks)[:, None] > jnp.arange(held_blocks)[None, :]
    slot_order = jnp.sum((earlier & (target[:, None] == target[None, :])).astype(jnp.int32), axis=1)
    slot_index = target * capacity + slot_order
    slot_hits = slot_index[None, :] == jnp.arange(slots, dtype=jnp.int32)[:, None]
    base_sent = jnp.sum(
        jnp.where(slot_hits[:, :, None], base_cells[None, :, :] + 1, 0), axis=1
    )
    arrived_base = lax.all_to_all(
        base_sent.reshape(devices, capacity * 2), "gz", split_axis=0, concat_axis=0, tiled=True
    )
    arrived_base = arrived_base.reshape(-1) - 1
    tables = marker_tables(marker_positions)
    boxes = pltpu.VMEM((slots, ROWS, 128), jnp.float32)
    grid = pltpu.VMEM((width, ROWS, 128), jnp.float32)
    packed = jax.ShapeDtypeStruct((slots * ROWS, 128), jnp.bfloat16)
    box_sent = local_call(build_kernel, packed, [SM, VM, VM], [boxes], "build")(
        slot_index, tables, marker_forces
    )
    arrived = lax.all_to_all(box_sent, "gz", split_axis=0, concat_axis=0, tiled=True)
    source = local_call(
        place_kernel,
        jax.ShapeDtypeStruct(fluid_source.shape, jnp.float32),
        [SM, VM, VM],
        [boxes, grid],
        "place",
    )(arrived_base, arrived, fluid_source)
    velocity = multigrid(source)
    picked = local_call(pick_kernel, packed, [SM, VM], [boxes, grid], "pick")(
        arrived_base, velocity
    )
    returned = lax.all_to_all(picked, "gz", split_axis=0, concat_axis=0, tiled=True)
    marker_velocity = local_call(
        read_kernel,
        jax.ShapeDtypeStruct(marker_positions.shape, jnp.float32),
        [SM, VM, VM],
        [boxes],
        "read",
    )(slot_index, tables, returned)
    return (velocity, marker_velocity)


def solution(mesh):
    placed = (
        P("gz", None, None),
        P("gz", None, None),
        P("gz", None),
        P("gz", None),
        P("gz", None, None, None),
    )
    return jax.shard_map(
        shards,
        mesh=mesh,
        in_specs=placed,
        out_specs=(P("gz", None, None, None), P("gz", None, None)),
        check_vma=False,
    )
```

```python
import functools
import math

import jax
import jax.numpy as jnp
from jax import lax
from jax.experimental import pallas as pl
from jax.experimental.pallas import tpu as pltpu
from jax.sharding import PartitionSpec as P

CZ = 4
BOX = 16
SWEEPS = 2
CSWEEPS = 6


screening = 1.0 / 64.0
relaxation = 2.0 / 3.0


def padded_2(array, sides, width):
    for axis, dim in sides:
        size, length = (lax.axis_size(axis), array.shape[dim])
        up = [(i, (i + 1) % size) for i in range(size)]
        down = [(j, i) for i, j in up]
        last = lax.slice_in_dim(array, length - width, length, axis=dim)
        initial = lax.slice_in_dim(array, 0, width, axis=dim)
        before = lax.ppermute(last, axis, up)
        after = lax.ppermute(initial, axis, down)
        array = jnp.concatenate([before, array, after], axis=dim)
    return array


ROWS = 2 * CZ * 3
HALF = CZ * 3
PACK = 8


def series(value, terms):
    total = jnp.full_like(value, terms[-1])
    for term in terms[-2::-1]:
        total = term + value * total
    return total


def marker_tables(positions):
    scale = jnp.array([BOX - 5.0, BOX - 5.0, CZ - 1.0], jnp.float32)[None, :, None]
    shift = jnp.array([2.0, 2.0, 0.0], jnp.float32)[None, :, None]
    place = shift + scale * positions
    nearest = jnp.floor(place + 0.5)
    turn = 0.5 * jnp.pi * (place - nearest)
    square = turn * turn
    cosine = series(square, [(-1.0) ** n / math.factorial(2 * n) for n in range(6)])
    sine = turn * series(square, [(-1.0) ** n / math.factorial(2 * n + 1) for n in range(6)])
    quarter = nearest.astype(jnp.int32) & 3
    odd = (quarter & 1) == 1
    along_cos = jnp.where(odd, sine, cosine)
    along_sin = jnp.where(odd, cosine, sine)
    along_cos = jnp.where((quarter == 1) | (quarter == 2), -along_cos, along_cos)
    along_sin = jnp.where(quarter >= 2, -along_sin, along_sin)
    return jnp.concatenate([place, along_cos, along_sin], axis=1)


def phi_rows(table, axis, cell):
    quarter = cell & 3
    along_cos = jnp.where(quarter == 0, 1.0, jnp.where(quarter == 2, -1.0, 0.0))
    along_sin = jnp.where(quarter == 1, 1.0, jnp.where(quarter == 3, -1.0, 0.0))
    offset = table[axis : axis + 1] - cell.astype(jnp.float32)
    wave = along_cos * table[3 + axis : 4 + axis] + along_sin * table[6 + axis : 7 + axis]
    return jnp.where(jnp.abs(offset) < 2.0, 0.25 + 0.25 * wave, 0.0)


def split_two(value):
    high = value.astype(jnp.bfloat16)
    return high, (value - high.astype(jnp.float32)).astype(jnp.bfloat16)


def block_weights(table):
    marks = table.shape[1]
    cell = lax.broadcasted_iota(jnp.int32, (BOX, marks), 0)
    weight_x = phi_rows(table, 0, cell)
    weight_y = phi_rows(table, 1, cell)
    weight_z = phi_rows(table, 2, cell & (CZ - 1))
    plane = (weight_x[:, None, :] * weight_y[None, :, :]).reshape(BOX * BOX, marks)
    return weight_z, split_two(plane)


def build_kernel(slot_ref, base_ref, table_ref, force_ref, out_ref, box_ref):
    blocks, marks = table_ref.shape[0], table_ref.shape[2]
    box_ref[...] = jnp.zeros_like(box_ref)

    def one(block):
        weight_z, (plane_high, plane_low) = block_weights(table_ref[block])
        force = force_ref[block]
        row = lax.broadcasted_iota(jnp.int32, (BOX, marks), 0)
        force = jnp.where(
            row < CZ,
            force[0:1],
            jnp.where(row < 2 * CZ, force[1:2], jnp.where(row < 3 * CZ, force[2:3], 0.0)),
        )
        loaded = jnp.concatenate(split_two(weight_z * force), axis=0)
        dims = (((1,), (1,)), ((), ()))
        both = lax.dot_general(loaded, plane_high, dims, preferred_element_type=jnp.float32)
        both = both + lax.dot_general(loaded, plane_low, dims, preferred_element_type=jnp.float32)
        box = both[:BOX] + both[BOX:]
        slot = slot_ref[block]
        near = box[:HALF, :128]
        tile_row = lax.broadcasted_iota(jnp.int32, near.shape, 0)
        lane = lax.broadcasted_iota(jnp.int32, near.shape, 1)
        first_x = base_ref[2 * block].astype(jnp.float32)
        first_y = base_ref[2 * block + 1].astype(jnp.float32)
        near = jnp.where((tile_row == 0) & (lane == 0), first_x, near)
        near = jnp.where((tile_row == 0) & (lane == 1), first_y, near)
        box_ref[slot, 0:HALF, :] = near
        box_ref[slot, HALF:ROWS, :] = box[:HALF, 128:]

    def some(turn, carry):
        for part in range(4):
            one(turn * 4 + part)
        return carry

    lax.fori_loop(0, blocks // 4, some, 0)
    pack_boxes(box_ref, out_ref)


def pack_boxes(box_ref, out_ref):
    def pack(turn, carry):
        boxes = box_ref[pl.ds(turn * PACK, PACK)]
        out_ref[pl.ds(pl.multiple_of(turn * PACK * ROWS, PACK * ROWS), PACK * ROWS), :] = (
            boxes.reshape(PACK * ROWS, 128).astype(jnp.bfloat16)
        )
        return carry

    lax.fori_loop(0, box_ref.shape[0] // PACK, pack, 0)


def unpack_boxes(in_ref, box_ref):
    def unpack(turn, carry):
        rows = in_ref[pl.ds(pl.multiple_of(turn * PACK * ROWS, PACK * ROWS), PACK * ROWS), :]
        box_ref[pl.ds(turn * PACK, PACK)] = rows.astype(jnp.float32).reshape(PACK, ROWS, 128)
        return carry

    lax.fori_loop(0, box_ref.shape[0] // PACK, unpack, 0)


def read_kernel(slot_ref, table_ref, in_ref, out_ref, box_ref):
    blocks = table_ref.shape[0]
    unpack_boxes(in_ref, box_ref)

    def one(block):
        weight_z, (plane_high, plane_low) = block_weights(table_ref[block])
        slot = slot_ref[block]
        first = box_ref[slot, 0:BOX, :]
        second = box_ref[slot, HALF - 4 : ROWS, :]
        second = pltpu.roll(second, BOX - 4, 0)
        box = jnp.concatenate([first, second], axis=1).astype(jnp.bfloat16)
        spread = jnp.dot(box, plane_high, preferred_element_type=jnp.float32)
        spread = spread + jnp.dot(box, plane_low, preferred_element_type=jnp.float32)
        spread = spread * weight_z
        for component in range(3):
            out_ref[block, component : component + 1, :] = jnp.sum(
                spread[component * CZ : (component + 1) * CZ], axis=0, keepdims=True
            )

    def some(turn, carry):
        for part in range(4):
            one(turn * 4 + part)
        return carry

    lax.fori_loop(0, blocks // 4, some, 0)


def place_kernel(base_ref, in_ref, fluid_ref, out_ref, box_ref, grid_ref, twin_ref):
    slots, width = box_ref.shape[0], fluid_ref.shape[2]
    unpack_boxes(in_ref, box_ref)
    grid_ref[...] = jnp.zeros_like(grid_ref)
    twin_ref[...] = jnp.zeros_like(twin_ref)
    lane = lax.broadcasted_iota(jnp.int32, (ROWS, 128), 1)
    row = lax.broadcasted_iota(jnp.int32, (ROWS, 128), 0)
    label = (row == 0) & (lane < 2)

    def moved_box(slot):
        first_x, first_y = base_ref[2 * slot], base_ref[2 * slot + 1]
        box = jnp.where(label, 0.0, box_ref[slot])
        inside = ((lane - first_y) & (width - 1)) < BOX
        pieces = []
        for step in range(8):
            moved = pltpu.roll(box, (first_y - BOX * step) & (width - 1), 1)
            pieces.append(((first_x + step) & (width - 1), jnp.where(inside, moved, 0.0)))
        return pieces

    def some(turn, carry):
        for part in range(2):
            even = moved_box(4 * turn + 2 * part)
            odd = moved_box(4 * turn + 2 * part + 1)
            for (x, piece), (other_x, other_piece) in zip(even, odd):
                grid_ref[x] += piece
                twin_ref[other_x] += other_piece
        return carry

    lax.fori_loop(0, slots // 4, some, 0)
    for layer in range(CZ):
        for component in range(3):
            row = component * CZ + layer
            near = grid_ref[:, row, :] + twin_ref[:, row, :]
            far = grid_ref[:, HALF + row, :] + twin_ref[:, HALF + row, :]
            far = pltpu.roll(far, 8, 0)
            out_ref[layer, component] = fluid_ref[layer, component] + (near + far)


def pick_kernel(base_ref, velocity_ref, out_ref, box_ref, grid_ref):
    slots, width = box_ref.shape[0], velocity_ref.shape[2]
    for layer in range(CZ):
        for component in range(3):
            row = component * CZ + layer
            low = velocity_ref[layer, component].astype(jnp.bfloat16).astype(jnp.float32)
            grid_ref[:, row, :] = low
            grid_ref[:, HALF + row, :] = pltpu.roll(low, width - 8, 0)
    lane = lax.broadcasted_iota(jnp.int32, (ROWS, 128), 1)

    def one(slot):
        first_x, first_y = base_ref[2 * slot], base_ref[2 * slot + 1]

        box = jnp.zeros((ROWS, 128), jnp.float32)
        for step in range(8):
            x = (first_x + step) & (width - 1)
            moved = pltpu.roll(grid_ref[x], (BOX * step - first_y) & (width - 1), 1)
            box = jnp.where(lane // BOX == step, moved, box)
        box_ref[slot] = box

    def some(turn, carry):
        for part in range(4):
            one(turn * 4 + part)
        return carry

    lax.fori_loop(0, slots // 4, some, 0)
    pack_boxes(box_ref, out_ref)


VM = pl.BlockSpec(memory_space=pltpu.VMEM)
SM = pl.BlockSpec(memory_space=pltpu.SMEM)


def local_call(body, out, specs, scratch, name):
    return pl.pallas_call(
        body,
        out_shape=out,
        in_specs=specs,
        out_specs=VM,
        scratch_shapes=scratch,
        name=name,
        compiler_params=pltpu.CompilerParams(vmem_limit_bytes=56 * 2**20),
    )


def factor_of(level):
    return relaxation / (screening + 6.0 * 0.25**level)


def split_three(value):
    high = value.astype(jnp.bfloat16)
    rest = value - high.astype(jnp.float32)
    middle = rest.astype(jnp.bfloat16)
    low = (rest - middle.astype(jnp.float32)).astype(jnp.bfloat16)
    return [high, middle, low]


def wide_dot(left, right):
    if right.dtype == jnp.bfloat16:
        parts = [jnp.dot(p, right, preferred_element_type=jnp.float32) for p in split_three(left)]
    else:
        parts = [jnp.dot(left, p, preferred_element_type=jnp.float32) for p in split_three(right)]
    return (parts[2] + parts[1]) + parts[0]


def table(rows, columns, rule):
    row = lax.broadcasted_iota(jnp.int32, (rows, columns), 0)
    column = lax.broadcasted_iota(jnp.int32, (rows, columns), 1)
    return jnp.where(rule(row, column), 1.0, 0.0).astype(jnp.bfloat16)


def beside(value, group_rows, group):
    axis = value.ndim - 2
    rows, lanes = value.shape[axis], value.shape[axis + 1]
    right = pltpu.roll(value, lanes - 1, axis + 1)
    left = pltpu.roll(value, 1, axis + 1)
    after = pltpu.roll(value, rows - 1, axis)
    before = pltpu.roll(value, 1, axis)
    if group < lanes:
        lane = lax.broadcasted_iota(jnp.int32, value.shape, axis + 1) & (group - 1)
        row = lax.broadcasted_iota(jnp.int32, value.shape, axis) & (group_rows - 1)
        right = jnp.where(lane == group - 1, pltpu.roll(value, group - 1, axis + 1), right)
        left = jnp.where(lane == 0, pltpu.roll(value, lanes - group + 1, axis + 1), left)
        wrap_after, wrap_before = after, before
        if group_rows < rows:
            wrap_after = pltpu.roll(value, group_rows - 1, axis)
            wrap_before = pltpu.roll(value, rows - group_rows + 1, axis)
        after = jnp.where(
            row == group_rows - 1, pltpu.roll(wrap_after, lanes - group, axis + 1), after
        )
        before = jnp.where(row == 0, pltpu.roll(wrap_before, group, axis + 1), before)
    return (right + left) + (after + before)


def first_sweep(source, around, level):
    factor = factor_of(level)
    return (4.0 / 3.0 * factor) * source + (factor * factor * 0.25**level) * around


def next_sweep(solution, source, around, level):
    factor = factor_of(level)
    return (1.0 - relaxation) * solution + factor * source + (factor * 0.25**level) * around


def left_over(solution, source, around, level):
    return source - (screening + 6.0 * 0.25**level) * solution + 0.25**level * around


def grid_kernel(
    devices,
    source_ref,
    out_ref,
    b0,
    u0,
    t0,
    b1,
    u1,
    t1,
    f1,
    b2,
    u2,
    send0,
    recv0,
    send1,
    recv1,
    send2,
    recv2,
):
    me = lax.axis_index("gz")

    def other(step):
        return lax.rem(me + step + devices, devices)

    barrier = pltpu.get_barrier_semaphore()

    def greet(step, carry):
        pl.semaphore_signal(
            barrier, inc=1, device_id=(other(step),), device_id_type=pl.DeviceIdType.MESH
        )
        return carry

    lax.fori_loop(1, devices, greet, 0)
    pl.semaphore_wait(barrier, devices - 1)

    def send(src, dst, send_sem, recv_sem, step):
        copy = pltpu.make_async_remote_copy(
            src_ref=src,
            dst_ref=dst,
            send_sem=send_sem,
            recv_sem=recv_sem,
            device_id=(other(step),),
            device_id_type=pl.DeviceIdType.MESH,
        )
        copy.start()
        return copy

    width, lanes = source_ref.shape[2], source_ref.shape[3]
    near = [
        send(source_ref.at[2:4], b0.at[1:3], send0.at[0], recv0.at[0], 1),
        send(source_ref.at[0:2], b0.at[7:9], send0.at[1], recv0.at[1], -1),
    ]
    far = [
        send(source_ref.at[1:2], b0.at[0:1], send0.at[2], recv0.at[2], 1),
        send(source_ref.at[2:3], b0.at[9:10], send0.at[3], recv0.at[3], -1),
    ]

    def loop(low, high, body):
        def step(turn, carry):
            for component in range(3):
                body(turn, component)
            return carry

        lax.fori_loop(low, high, step, 0)

    def keep(z, c):
        b0[z + 3, c] = source_ref[z, c]

    loop(0, 4, keep)

    def begin0(z, c):
        here = b0[z, c]
        around = beside(here, width, lanes) + (b0[z - 1, c] + b0[z + 1, c])
        u0[z - 1, c] = first_sweep(here, around, 0)

    loop(4, 6, begin0)
    for copy in near:
        copy.wait()
    loop(2, 4, begin0)
    loop(6, 8, begin0)

    half = width // 2
    fold0 = table(half, width, lambda r, c: c // 2 == r)
    pack0 = [
        table(lanes, lanes, lambda r, c, a=a: (c // half == a) & (r // 2 == c % half))
        for a in range(2)
    ]
    quarter = half // 2
    fold1 = table(quarter // 2, quarter, lambda r, c: c // 2 == r)
    rows1, rows2 = quarter, quarter // 4
    group1, group2 = half, quarter

    def rest0(z, c):
        here = u0[z + 2, c]
        around = beside(here, width, lanes) + (u0[z + 1, c] + u0[z + 3, c])
        return left_over(here, b0[z + 3, c], around, 0)

    def down0(z1, c):
        pair = 0.125 * (rest0(2 * z1, c) + rest0(2 * z1 + 1, c))
        folded = wide_dot(fold0, pair)
        b1[z1 + 4, c] = wide_dot(folded[:rows1], pack0[0]) + wide_dot(folded[rows1:], pack0[1])

    loop(0, 2, down0)
    near1 = [
        send(b1.at[4:6], b1.at[2:4], send1.at[0], recv1.at[0], 1),
        send(b1.at[4:6], b1.at[6:8], send1.at[1], recv1.at[1], -1),
    ]
    far1 = [
        send(b1.at[4:6], b1.at[0:2], send1.at[2], recv1.at[2], 2),
        send(b1.at[4:6], b1.at[8:10], send1.at[3], recv1.at[3], -2),
    ]

    def begin1(z, c):
        here = b1[z, c]
        around = beside(here, rows1, group1) + (b1[z - 1, c] + b1[z + 1, c])
        u1[z - 1, c] = first_sweep(here, around, 1)

    for copy in near1:
        copy.wait()
    loop(3, 7, begin1)

    def rest1(z, c):
        here = u1[z + 3, c]
        around = beside(here, rows1, group1) + (u1[z + 2, c] + u1[z + 4, c])
        return left_over(here, b1[z + 4, c], around, 1)

    pack1 = [
        table(
            lanes,
            lanes,
            lambda r, c, a=a: (c // group2 == 2 * (r // group1) + a)
            & (c % group2 == (r % group1) // 2),
        )
        for a in range(2)
    ]
    for c in range(3):
        folded = wide_dot(fold1, 0.125 * (rest1(0, c) + rest1(1, c)))
        b2[me, c] = wide_dot(folded[:rows2], pack1[0]) + wide_dot(folded[rows2:], pack1[1])

    def spread(step, carry):
        send(b2.at[me], b2.at[me], send2, recv2, step)
        return carry

    lax.fori_loop(1, devices, spread, 0)
    for copy in far:
        copy.wait()
    loop(1, 2, begin0)
    loop(8, 9, begin0)
    for copy in far1:
        copy.wait()
    loop(1, 3, begin1)
    loop(7, 9, begin1)
    rest = b2.at[0 : devices - 1]
    pltpu.make_async_copy(rest, rest, send2).wait()
    pltpu.make_async_copy(rest, rest, recv2).wait()

    count = 3 * devices
    half2 = devices // 2
    group3 = group2 // 2
    rhs2 = b2[...].reshape(count, rows2, lanes)

    def around2(value):
        ends = jnp.concatenate([value[3:], value[:3]], 0) + jnp.concatenate(
            [value[-3:], value[:-3]], 0
        )
        return beside(value, rows2, group2) + ends

    sol2 = first_sweep(rhs2, around2(rhs2), 2)
    left2 = left_over(sol2, rhs2, around2(sol2), 2).reshape(half2, 2, 3 * rows2, lanes)
    left2 = (0.125 * (left2[:, 0] + left2[:, 1])).reshape(half2 * 3 * rows2, lanes)
    span3 = 4 * group3
    pack2 = table(
        lanes,
        lanes,
        lambda r, c: ((c % span3) // group3 == r // group2) & (c % group3 == (r % group2) // 2),
    )
    rows3 = rows2 // 2
    fold2 = table(
        4 * rows3,
        3 * rows2,
        lambda r, c: (c // rows2 == r // rows3) & ((c % rows2) // 2 == r % rows3),
    )
    left2 = wide_dot(left2, pack2).reshape(half2, 3 * rows2, lanes)
    rhs3 = jnp.stack([wide_dot(fold2, left2[z]) for z in range(half2)], 0)

    def around3(value):
        ends = jnp.concatenate([value[1:], value[:1]], 0) + jnp.concatenate(
            [value[-1:], value[:-1]], 0
        )
        return beside(value, rows3, group3) + ends

    sol3 = first_sweep(rhs3, around3(rhs3), 3)
    for turn in range(CSWEEPS - 2):
        sol3 = next_sweep(sol3, rhs3, around3(sol3), 3)
    total = jnp.sum(left_over(sol3, rhs3, around3(sol3), 3), axis=0)
    total = jnp.broadcast_to(jnp.sum(total, axis=1, keepdims=True), total.shape)
    same = table(4 * rows3, 4 * rows3, lambda r, c: r // rows3 == c // rows3)
    cells = half2 * rows3 * lanes
    sol3 = sol3 + (wide_dot(same, total) * (1.0 / (screening * cells)))[None]

    open2 = table(
        lanes,
        lanes,
        lambda r, c: (r < span3)
        & (r // group3 == c // group2)
        & (r % group3 == (c % group2) // 2),
    )
    rise2 = table(
        3 * rows2,
        4 * rows3,
        lambda r, c: (r // rows2 == c // rows3) & ((r % rows2) // 2 == c % rows3),
    )
    lift = jnp.concatenate([wide_dot(rise2, sol3[z]) for z in range(half2)], 0)
    lift = wide_dot(lift, open2).reshape(half2, 1, 3 * rows2, lanes)
    lift = jnp.concatenate([lift, lift], axis=1).reshape(count, rows2, lanes)
    sol2 = sol2 + lift
    for turn in range(SWEEPS):
        sol2 = next_sweep(sol2, rhs2, around2(sol2), 2)
    u2[...] = sol2.reshape(devices, 3, rows2, lanes)

    rise1 = table(quarter, quarter // 2, lambda r, c: r // 2 == c)
    open1 = [
        table(
            lanes,
            lanes,
            lambda r, c, a=a: (r // group2 == 2 * (c // group1) + a)
            & (r % group2 == (c % group1) // 2),
        )
        for a in range(2)
    ]

    def lift1(z2, c):
        coarse = u2[other(z2 - 2), c]
        tall = jnp.concatenate([wide_dot(coarse, open1[0]), wide_dot(coarse, open1[1])], 0)
        return wide_dot(rise1, tall)

    for c in range(3):
        u1[0, c] += lift1(0, c)
        u1[7, c] += lift1(4, c)

    def raise1(z2, c):
        up = lift1(z2, c)
        u1[2 * z2 - 1, c] += up
        u1[2 * z2, c] += up

    loop(1, 4, raise1)

    def later1(z, c):
        here = u1[z, c]
        around = beside(here, rows1, group1) + (u1[z - 1, c] + u1[z + 1, c])
        t1[z - 1, c] = next_sweep(here, b1[z + 1, c], around, 1)

    loop(1, 7, later1)

    def last1(z, c):
        here = t1[z, c]
        around = beside(here, rows1, group1) + (t1[z - 1, c] + t1[z + 1, c])
        f1[z - 1, c] = next_sweep(here, b1[z + 2, c], around, 1)

    loop(1, 5, last1)

    rise0 = table(width, half, lambda r, c: r // 2 == c)
    open0 = [
        table(lanes, lanes, lambda r, c, a=a: (r // half == a) & (c // 2 == r % half))
        for a in range(2)
    ]

    def raise0(z1, c):
        coarse = f1[z1, c]
        tall = jnp.concatenate([wide_dot(coarse, open0[0]), wide_dot(coarse, open0[1])], 0)
        up = wide_dot(rise0, tall)
        u0[2 * z1, c] += up
        u0[2 * z1 + 1, c] += up

    loop(0, 4, raise0)

    def later0(z, c):
        here = u0[z, c]
        around = beside(here, width, lanes) + (u0[z - 1, c] + u0[z + 1, c])
        t0[z - 1, c] = next_sweep(here, b0[z + 1, c], around, 0)

    loop(1, 7, later0)

    def last0(z, c):
        here = t0[z, c]
        around = beside(here, width, lanes) + (t0[z - 1, c] + t0[z + 1, c])
        out_ref[z - 1, c] = next_sweep(here, b0[z + 2, c], around, 0)

    loop(1, 5, last0)


def multigrid(source):
    devices = lax.axis_size("gz")
    width = source.shape[3]
    fine, middle, third = (3, width, width), (3, width // 4, width), (3, width // 16, width)
    dma = pltpu.SemaphoreType.DMA
    scratch = [
        pltpu.VMEM((10,) + fine, jnp.float32),
        pltpu.VMEM((8,) + fine, jnp.float32),
        pltpu.VMEM((6,) + fine, jnp.float32),
        pltpu.VMEM((10,) + middle, jnp.float32),
        pltpu.VMEM((8,) + middle, jnp.float32),
        pltpu.VMEM((6,) + middle, jnp.float32),
        pltpu.VMEM((4,) + middle, jnp.float32),
        pltpu.VMEM((devices,) + third, jnp.float32),
        pltpu.VMEM((devices,) + third, jnp.float32),
        dma((4,)),
        dma((4,)),
        dma((4,)),
        dma((4,)),
        dma,
        dma,
    ]
    return pl.pallas_call(
        functools.partial(grid_kernel, devices),
        out_shape=jax.ShapeDtypeStruct(source.shape, jnp.float32),
        in_specs=[VM],
        out_specs=VM,
        scratch_shapes=scratch,
        name="multigrid",
        compiler_params=pltpu.CompilerParams(
            collective_id=0, has_side_effects=True, vmem_limit_bytes=56 * 2**20
        ),
    )(source)


def shards(marker_positions, marker_forces, dest_slab, base_cells, fluid_source):
    devices = lax.axis_size("gz")
    held_blocks = marker_positions.shape[0]
    width = fluid_source.shape[2]
    capacity = max(2, 2 * held_blocks // devices)
    slots = devices * capacity
    target = dest_slab[:, 0]
    earlier = jnp.arange(held_blocks)[:, None] > jnp.arange(held_blocks)[None, :]
    slot_order = jnp.sum((earlier & (target[:, None] == target[None, :])).astype(jnp.int32), axis=1)
    slot_index = target * capacity + slot_order
    tables = marker_tables(marker_positions)
    boxes = pltpu.VMEM((slots, ROWS, 128), jnp.float32)
    grid = pltpu.VMEM((width, ROWS, 128), jnp.float32)
    packed = jax.ShapeDtypeStruct((slots * ROWS, 128), jnp.bfloat16)
    box_sent = local_call(build_kernel, packed, [SM, SM, VM, VM], [boxes], "build")(
        slot_index, base_cells.reshape(-1), tables, marker_forces
    )
    arrived = lax.all_to_all(box_sent, "gz", split_axis=0, concat_axis=0, tiled=True)
    labels = lax.slice(arrived.reshape(slots, ROWS, 128), (0, 0, 0), (slots, 1, 2))
    arrived_base = labels.reshape(-1).astype(jnp.int32)
    source = local_call(
        place_kernel,
        jax.ShapeDtypeStruct(fluid_source.shape, jnp.float32),
        [SM, VM, VM],
        [boxes, grid, grid],
        "place",
    )(arrived_base, arrived, fluid_source)
    velocity = multigrid(source)
    picked = local_call(pick_kernel, packed, [SM, VM], [boxes, grid], "pick")(
        arrived_base, velocity
    )
    returned = lax.all_to_all(picked, "gz", split_axis=0, concat_axis=0, tiled=True)
    marker_velocity = local_call(
        read_kernel,
        jax.ShapeDtypeStruct(marker_positions.shape, jnp.float32),
        [SM, VM, VM],
        [boxes],
        "read",
    )(slot_index, tables, returned)
    return (velocity, marker_velocity)


def solution(mesh):
    placed = (
        P("gz", None, None),
        P("gz", None, None),
        P("gz", None),
        P("gz", None),
        P("gz", None, None, None),
    )
    return jax.shard_map(
        shards,
        mesh=mesh,
        in_specs=placed,
        out_specs=(P("gz", None, None, None), P("gz", None, None)),
        check_vma=False,
    )
```

```python
import functools
import math

import jax
import jax.numpy as jnp
from jax import lax
from jax.experimental import pallas as pl
from jax.experimental.pallas import tpu as pltpu
from jax.sharding import PartitionSpec as P

CZ = 4
BOX = 16
SWEEPS = 2
CSWEEPS = 6


screening = 1.0 / 64.0
relaxation = 2.0 / 3.0


def padded_2(array, sides, width):
    for axis, dim in sides:
        size, length = (lax.axis_size(axis), array.shape[dim])
        up = [(i, (i + 1) % size) for i in range(size)]
        down = [(j, i) for i, j in up]
        last = lax.slice_in_dim(array, length - width, length, axis=dim)
        initial = lax.slice_in_dim(array, 0, width, axis=dim)
        before = lax.ppermute(last, axis, up)
        after = lax.ppermute(initial, axis, down)
        array = jnp.concatenate([before, array, after], axis=dim)
    return array


ROWS = 2 * CZ * 3
HALF = CZ * 3
PACK = 8


def series(value, terms):
    total = jnp.full_like(value, terms[-1])
    for term in terms[-2::-1]:
        total = term + value * total
    return total


def marker_tables(positions):
    scale = jnp.array([BOX - 5.0, BOX - 5.0, CZ - 1.0], jnp.float32)[None, :, None]
    shift = jnp.array([2.0, 2.0, 0.0], jnp.float32)[None, :, None]
    place = shift + scale * positions
    nearest = jnp.floor(place + 0.5)
    turn = 0.5 * jnp.pi * (place - nearest)
    square = turn * turn
    cosine = series(square, [(-1.0) ** n / math.factorial(2 * n) for n in range(6)])
    sine = turn * series(square, [(-1.0) ** n / math.factorial(2 * n + 1) for n in range(6)])
    quarter = nearest.astype(jnp.int32) & 3
    odd = (quarter & 1) == 1
    along_cos = jnp.where(odd, sine, cosine)
    along_sin = jnp.where(odd, cosine, sine)
    along_cos = jnp.where((quarter == 1) | (quarter == 2), -along_cos, along_cos)
    along_sin = jnp.where(quarter >= 2, -along_sin, along_sin)
    return jnp.concatenate([place, along_cos, along_sin], axis=1)


def phi_rows(table, axis, cell):
    quarter = cell & 3
    along_cos = jnp.where(quarter == 0, 1.0, jnp.where(quarter == 2, -1.0, 0.0))
    along_sin = jnp.where(quarter == 1, 1.0, jnp.where(quarter == 3, -1.0, 0.0))
    offset = table[axis : axis + 1] - cell.astype(jnp.float32)
    wave = along_cos * table[3 + axis : 4 + axis] + along_sin * table[6 + axis : 7 + axis]
    return jnp.where(jnp.abs(offset) < 2.0, 0.25 + 0.25 * wave, 0.0)


def split_two(value):
    high = value.astype(jnp.bfloat16)
    return high, (value - high.astype(jnp.float32)).astype(jnp.bfloat16)


def block_weights(table):
    marks = table.shape[1]
    cell = lax.broadcasted_iota(jnp.int32, (BOX, marks), 0)
    weight_x = phi_rows(table, 0, cell)
    weight_y = phi_rows(table, 1, cell)
    weight_z = phi_rows(table, 2, cell & (CZ - 1))
    plane = (weight_x[:, None, :] * weight_y[None, :, :]).reshape(BOX * BOX, marks)
    return weight_z, split_two(plane)


def build_kernel(slot_ref, base_ref, table_ref, force_ref, out_ref, box_ref):
    blocks, marks = table_ref.shape[0], table_ref.shape[2]
    box_ref[...] = jnp.zeros_like(box_ref)

    def one(block):
        weight_z, (plane_high, plane_low) = block_weights(table_ref[block])
        force = force_ref[block]
        row = lax.broadcasted_iota(jnp.int32, (BOX, marks), 0)
        force = jnp.where(
            row < CZ,
            force[0:1],
            jnp.where(row < 2 * CZ, force[1:2], jnp.where(row < 3 * CZ, force[2:3], 0.0)),
        )
        loaded = jnp.concatenate(split_two(weight_z * force), axis=0)
        dims = (((1,), (1,)), ((), ()))
        both = lax.dot_general(loaded, plane_high, dims, preferred_element_type=jnp.float32)
        both = both + lax.dot_general(loaded, plane_low, dims, preferred_element_type=jnp.float32)
        box = both[:BOX] + both[BOX:]
        slot = slot_ref[block]
        near = box[:HALF, :128]
        tile_row = lax.broadcasted_iota(jnp.int32, near.shape, 0)
        lane = lax.broadcasted_iota(jnp.int32, near.shape, 1)
        first_x = base_ref[2 * block].astype(jnp.float32)
        first_y = base_ref[2 * block + 1].astype(jnp.float32)
        near = jnp.where((tile_row == 0) & (lane == 0), first_x, near)
        near = jnp.where((tile_row == 0) & (lane == 1), first_y, near)
        box_ref[slot, 0:HALF, :] = near
        box_ref[slot, HALF:ROWS, :] = box[:HALF, 128:]

    def some(turn, carry):
        for part in range(4):
            one(turn * 4 + part)
        return carry

    lax.fori_loop(0, blocks // 4, some, 0)
    pack_boxes(box_ref, out_ref)


def pack_boxes(box_ref, out_ref):
    def pack(turn, carry):
        boxes = box_ref[pl.ds(turn * PACK, PACK)]
        out_ref[pl.ds(pl.multiple_of(turn * PACK * ROWS, PACK * ROWS), PACK * ROWS), :] = (
            boxes.reshape(PACK * ROWS, 128).astype(jnp.bfloat16)
        )
        return carry

    lax.fori_loop(0, box_ref.shape[0] // PACK, pack, 0)


def unpack_boxes(in_ref, box_ref):
    def unpack(turn, carry):
        rows = in_ref[pl.ds(pl.multiple_of(turn * PACK * ROWS, PACK * ROWS), PACK * ROWS), :]
        box_ref[pl.ds(turn * PACK, PACK)] = rows.astype(jnp.float32).reshape(PACK, ROWS, 128)
        return carry

    lax.fori_loop(0, box_ref.shape[0] // PACK, unpack, 0)


def read_kernel(slot_ref, table_ref, in_ref, out_ref, box_ref):
    blocks = table_ref.shape[0]
    unpack_boxes(in_ref, box_ref)

    def one(block):
        weight_z, (plane_high, plane_low) = block_weights(table_ref[block])
        slot = slot_ref[block]
        first = box_ref[slot, 0:BOX, :]
        second = box_ref[slot, HALF - 4 : ROWS, :]
        second = pltpu.roll(second, BOX - 4, 0)
        box = jnp.concatenate([first, second], axis=1).astype(jnp.bfloat16)
        spread = jnp.dot(box, plane_high, preferred_element_type=jnp.float32)
        spread = spread + jnp.dot(box, plane_low, preferred_element_type=jnp.float32)
        spread = spread * weight_z
        for component in range(3):
            out_ref[block, component : component + 1, :] = jnp.sum(
                spread[component * CZ : (component + 1) * CZ], axis=0, keepdims=True
            )

    def some(turn, carry):
        for part in range(4):
            one(turn * 4 + part)
        return carry

    lax.fori_loop(0, blocks // 4, some, 0)


def rows_of(x):
    return pl.ds(pl.multiple_of(x * ROWS, 8), ROWS)


def place_kernel(base_ref, in_ref, fluid_ref, out_ref, box_ref, grid_ref, twin_ref):
    slots, width = box_ref.shape[0], fluid_ref.shape[2]
    unpack_boxes(in_ref, box_ref)
    grid_ref[...] = jnp.zeros_like(grid_ref)
    twin_ref[...] = jnp.zeros_like(twin_ref)
    lane = lax.broadcasted_iota(jnp.int32, (ROWS, 128), 1)
    row = lax.broadcasted_iota(jnp.int32, (ROWS, 128), 0)
    label = (row == 0) & (lane < 2)

    def moved_box(slot):
        first_x, first_y = base_ref[2 * slot], base_ref[2 * slot + 1]
        box = jnp.where(label, 0.0, box_ref[slot])
        inside = ((lane - first_y) & (width - 1)) < BOX
        pieces = []
        for step in range(8):
            moved = pltpu.roll(box, (first_y - BOX * step) & (width - 1), 1)
            pieces.append(((first_x + step) & (width - 1), jnp.where(inside, moved, 0.0)))
        return pieces

    def some(turn, carry):
        for part in range(2):
            even = moved_box(4 * turn + 2 * part)
            odd = moved_box(4 * turn + 2 * part + 1)
            for (x, piece), (other_x, other_piece) in zip(even, odd):
                grid_ref[rows_of(x), :] += piece
                twin_ref[rows_of(other_x), :] += other_piece
        return carry

    lax.fori_loop(0, slots // 4, some, 0)
    for layer in range(CZ):
        for component in range(3):
            row = component * CZ + layer
            near_rows = pl.ds(row, width, stride=ROWS)
            far_rows = pl.ds(HALF + row, width, stride=ROWS)
            near = grid_ref[near_rows, :] + twin_ref[near_rows, :]
            far = grid_ref[far_rows, :] + twin_ref[far_rows, :]
            far = pltpu.roll(far, 8, 0)
            out_ref[layer, component] = fluid_ref[layer, component] + (near + far)


def pick_kernel(base_ref, velocity_ref, out_ref, box_ref, grid_ref):
    slots, width = box_ref.shape[0], velocity_ref.shape[2]
    for layer in range(CZ):
        for component in range(3):
            row = component * CZ + layer
            low = velocity_ref[layer, component].astype(jnp.bfloat16).astype(jnp.float32)
            grid_ref[pl.ds(row, width, stride=ROWS), :] = low
            grid_ref[pl.ds(HALF + row, width, stride=ROWS), :] = pltpu.roll(low, width - 8, 0)
    lane = lax.broadcasted_iota(jnp.int32, (ROWS, 128), 1)

    def one(slot):
        first_x, first_y = base_ref[2 * slot], base_ref[2 * slot + 1]

        box = jnp.zeros((ROWS, 128), jnp.float32)
        for step in range(8):
            x = (first_x + step) & (width - 1)
            moved = pltpu.roll(grid_ref[rows_of(x), :], (BOX * step - first_y) & (width - 1), 1)
            box = jnp.where(lane // BOX == step, moved, box)
        box_ref[slot] = box

    def some(turn, carry):
        for part in range(4):
            one(turn * 4 + part)
        return carry

    lax.fori_loop(0, slots // 4, some, 0)
    pack_boxes(box_ref, out_ref)


VM = pl.BlockSpec(memory_space=pltpu.VMEM)
SM = pl.BlockSpec(memory_space=pltpu.SMEM)


def local_call(body, out, specs, scratch, name):
    return pl.pallas_call(
        body,
        out_shape=out,
        in_specs=specs,
        out_specs=VM,
        scratch_shapes=scratch,
        name=name,
        compiler_params=pltpu.CompilerParams(vmem_limit_bytes=56 * 2**20),
    )


def factor_of(level):
    return relaxation / (screening + 6.0 * 0.25**level)


def split_three(value):
    high = value.astype(jnp.bfloat16)
    rest = value - high.astype(jnp.float32)
    middle = rest.astype(jnp.bfloat16)
    low = (rest - middle.astype(jnp.float32)).astype(jnp.bfloat16)
    return [high, middle, low]


def wide_dot(left, right):
    if right.dtype == jnp.bfloat16:
        parts = [jnp.dot(p, right, preferred_element_type=jnp.float32) for p in split_three(left)]
    else:
        parts = [jnp.dot(left, p, preferred_element_type=jnp.float32) for p in split_three(right)]
    return (parts[2] + parts[1]) + parts[0]


def table(rows, columns, rule):
    row = lax.broadcasted_iota(jnp.int32, (rows, columns), 0)
    column = lax.broadcasted_iota(jnp.int32, (rows, columns), 1)
    return jnp.where(rule(row, column), 1.0, 0.0).astype(jnp.bfloat16)


def beside(value, group_rows, group):
    axis = value.ndim - 2
    rows, lanes = value.shape[axis], value.shape[axis + 1]
    right = pltpu.roll(value, lanes - 1, axis + 1)
    left = pltpu.roll(value, 1, axis + 1)
    after = pltpu.roll(value, rows - 1, axis)
    before = pltpu.roll(value, 1, axis)
    if group < lanes:
        lane = lax.broadcasted_iota(jnp.int32, value.shape, axis + 1) & (group - 1)
        row = lax.broadcasted_iota(jnp.int32, value.shape, axis) & (group_rows - 1)
        right = jnp.where(lane == group - 1, pltpu.roll(value, group - 1, axis + 1), right)
        left = jnp.where(lane == 0, pltpu.roll(value, lanes - group + 1, axis + 1), left)
        wrap_after, wrap_before = after, before
        if group_rows < rows:
            wrap_after = pltpu.roll(value, group_rows - 1, axis)
            wrap_before = pltpu.roll(value, rows - group_rows + 1, axis)
        after = jnp.where(
            row == group_rows - 1, pltpu.roll(wrap_after, lanes - group, axis + 1), after
        )
        before = jnp.where(row == 0, pltpu.roll(wrap_before, group, axis + 1), before)
    return (right + left) + (after + before)


def first_sweep(source, around, level):
    factor = factor_of(level)
    return (4.0 / 3.0 * factor) * source + (factor * factor * 0.25**level) * around


def next_sweep(solution, source, around, level):
    factor = factor_of(level)
    return (1.0 - relaxation) * solution + factor * source + (factor * 0.25**level) * around


def left_over(solution, source, around, level):
    return source - (screening + 6.0 * 0.25**level) * solution + 0.25**level * around


def grid_kernel(
    devices,
    source_ref,
    out_ref,
    b0,
    u0,
    t0,
    b1,
    u1,
    t1,
    f1,
    b2,
    u2,
    send0,
    recv0,
    send1,
    recv1,
    send2,
    recv2,
):
    me = lax.axis_index("gz")

    def other(step):
        return lax.rem(me + step + devices, devices)

    barrier = pltpu.get_barrier_semaphore()

    def greet(step, carry):
        pl.semaphore_signal(
            barrier, inc=1, device_id=(other(step),), device_id_type=pl.DeviceIdType.MESH
        )
        return carry

    lax.fori_loop(1, devices, greet, 0)
    pl.semaphore_wait(barrier, devices - 1)

    def send(src, dst, send_sem, recv_sem, step):
        copy = pltpu.make_async_remote_copy(
            src_ref=src,
            dst_ref=dst,
            send_sem=send_sem,
            recv_sem=recv_sem,
            device_id=(other(step),),
            device_id_type=pl.DeviceIdType.MESH,
        )
        copy.start()
        return copy

    width, lanes = source_ref.shape[2], source_ref.shape[3]
    near = [
        send(source_ref.at[2:4], b0.at[1:3], send0.at[0], recv0.at[0], 1),
        send(source_ref.at[0:2], b0.at[7:9], send0.at[1], recv0.at[1], -1),
    ]
    far = [
        send(source_ref.at[1:2], b0.at[0:1], send0.at[2], recv0.at[2], 1),
        send(source_ref.at[2:3], b0.at[9:10], send0.at[3], recv0.at[3], -1),
    ]

    def loop(low, high, body):
        def step(turn, carry):
            for component in range(3):
                body(turn, component)
            return carry

        lax.fori_loop(low, high, step, 0, unroll=True)

    def keep(z, c):
        b0[z + 3, c] = source_ref[z, c]

    loop(0, 4, keep)

    def begin0(z, c):
        here = b0[z, c]
        around = beside(here, width, lanes) + (b0[z - 1, c] + b0[z + 1, c])
        u0[z - 1, c] = first_sweep(here, around, 0)

    loop(4, 6, begin0)
    for copy in near:
        copy.wait()
    loop(2, 4, begin0)
    loop(6, 8, begin0)

    half = width // 2
    fold0 = table(half, width, lambda r, c: c // 2 == r)
    pack0 = [
        table(lanes, lanes, lambda r, c, a=a: (c // half == a) & (r // 2 == c % half))
        for a in range(2)
    ]
    quarter = half // 2
    fold1 = table(quarter // 2, quarter, lambda r, c: c // 2 == r)
    rows1, rows2 = quarter, quarter // 4
    group1, group2 = half, quarter

    def rest0(z, c):
        here = u0[z + 2, c]
        around = beside(here, width, lanes) + (u0[z + 1, c] + u0[z + 3, c])
        return left_over(here, b0[z + 3, c], around, 0)

    def down0(z1, c):
        pair = 0.125 * (rest0(2 * z1, c) + rest0(2 * z1 + 1, c))
        folded = wide_dot(fold0, pair)
        b1[z1 + 4, c] = wide_dot(folded[:rows1], pack0[0]) + wide_dot(folded[rows1:], pack0[1])

    loop(0, 2, down0)
    near1 = [
        send(b1.at[4:6], b1.at[2:4], send1.at[0], recv1.at[0], 1),
        send(b1.at[4:6], b1.at[6:8], send1.at[1], recv1.at[1], -1),
    ]
    far1 = [
        send(b1.at[4:6], b1.at[0:2], send1.at[2], recv1.at[2], 2),
        send(b1.at[4:6], b1.at[8:10], send1.at[3], recv1.at[3], -2),
    ]

    def begin1(z, c):
        here = b1[z, c]
        around = beside(here, rows1, group1) + (b1[z - 1, c] + b1[z + 1, c])
        u1[z - 1, c] = first_sweep(here, around, 1)

    for copy in near1:
        copy.wait()
    loop(3, 7, begin1)

    def rest1(z, c):
        here = u1[z + 3, c]
        around = beside(here, rows1, group1) + (u1[z + 2, c] + u1[z + 4, c])
        return left_over(here, b1[z + 4, c], around, 1)

    pack1 = [
        table(
            lanes,
            lanes,
            lambda r, c, a=a: (c // group2 == 2 * (r // group1) + a)
            & (c % group2 == (r % group1) // 2),
        )
        for a in range(2)
    ]
    for c in range(3):
        folded = wide_dot(fold1, 0.125 * (rest1(0, c) + rest1(1, c)))
        b2[me, c] = wide_dot(folded[:rows2], pack1[0]) + wide_dot(folded[rows2:], pack1[1])

    def spread(step, carry):
        send(b2.at[me], b2.at[me], send2, recv2, step)
        return carry

    lax.fori_loop(1, devices, spread, 0)
    for copy in far:
        copy.wait()
    loop(1, 2, begin0)
    loop(8, 9, begin0)
    for copy in far1:
        copy.wait()
    loop(1, 3, begin1)
    loop(7, 9, begin1)
    rest = b2.at[0 : devices - 1]
    pltpu.make_async_copy(rest, rest, send2).wait()
    pltpu.make_async_copy(rest, rest, recv2).wait()

    count = 3 * devices
    half2 = devices // 2
    group3 = group2 // 2
    rhs2 = b2[...].reshape(count, rows2, lanes)

    def around2(value):
        ends = jnp.concatenate([value[3:], value[:3]], 0) + jnp.concatenate(
            [value[-3:], value[:-3]], 0
        )
        return beside(value, rows2, group2) + ends

    sol2 = first_sweep(rhs2, around2(rhs2), 2)
    left2 = left_over(sol2, rhs2, around2(sol2), 2).reshape(half2, 2, 3 * rows2, lanes)
    left2 = (0.125 * (left2[:, 0] + left2[:, 1])).reshape(half2 * 3 * rows2, lanes)
    span3 = 4 * group3
    pack2 = table(
        lanes,
        lanes,
        lambda r, c: ((c % span3) // group3 == r // group2) & (c % group3 == (r % group2) // 2),
    )
    rows3 = rows2 // 2
    fold2 = table(
        4 * rows3,
        3 * rows2,
        lambda r, c: (c // rows2 == r // rows3) & ((c % rows2) // 2 == r % rows3),
    )
    left2 = wide_dot(left2, pack2).reshape(half2, 3 * rows2, lanes)
    rhs3 = jnp.stack([wide_dot(fold2, left2[z]) for z in range(half2)], 0)

    def around3(value):
        ends = jnp.concatenate([value[1:], value[:1]], 0) + jnp.concatenate(
            [value[-1:], value[:-1]], 0
        )
        return beside(value, rows3, group3) + ends

    sol3 = first_sweep(rhs3, around3(rhs3), 3)
    for turn in range(CSWEEPS - 2):
        sol3 = next_sweep(sol3, rhs3, around3(sol3), 3)
    total = jnp.sum(left_over(sol3, rhs3, around3(sol3), 3), axis=0)
    total = jnp.broadcast_to(jnp.sum(total, axis=1, keepdims=True), total.shape)
    same = table(4 * rows3, 4 * rows3, lambda r, c: r // rows3 == c // rows3)
    cells = half2 * rows3 * lanes
    sol3 = sol3 + (wide_dot(same, total) * (1.0 / (screening * cells)))[None]

    open2 = table(
        lanes,
        lanes,
        lambda r, c: (r < span3)
        & (r // group3 == c // group2)
        & (r % group3 == (c % group2) // 2),
    )
    rise2 = table(
        3 * rows2,
        4 * rows3,
        lambda r, c: (r // rows2 == c // rows3) & ((r % rows2) // 2 == c % rows3),
    )
    lift = jnp.concatenate([wide_dot(rise2, sol3[z]) for z in range(half2)], 0)
    lift = wide_dot(lift, open2).reshape(half2, 1, 3 * rows2, lanes)
    lift = jnp.concatenate([lift, lift], axis=1).reshape(count, rows2, lanes)
    sol2 = sol2 + lift
    for turn in range(SWEEPS):
        sol2 = next_sweep(sol2, rhs2, around2(sol2), 2)
    u2[...] = sol2.reshape(devices, 3, rows2, lanes)

    rise1 = table(quarter, quarter // 2, lambda r, c: r // 2 == c)
    open1 = [
        table(
            lanes,
            lanes,
            lambda r, c, a=a: (r // group2 == 2 * (c // group1) + a)
            & (r % group2 == (c % group1) // 2),
        )
        for a in range(2)
    ]

    def lift1(z2, c):
        coarse = u2[other(z2 - 2), c]
        tall = jnp.concatenate([wide_dot(coarse, open1[0]), wide_dot(coarse, open1[1])], 0)
        return wide_dot(rise1, tall)

    for c in range(3):
        u1[0, c] += lift1(0, c)
        u1[7, c] += lift1(4, c)

    def raise1(z2, c):
        up = lift1(z2, c)
        u1[2 * z2 - 1, c] += up
        u1[2 * z2, c] += up

    loop(1, 4, raise1)

    def later1(z, c):
        here = u1[z, c]
        around = beside(here, rows1, group1) + (u1[z - 1, c] + u1[z + 1, c])
        t1[z - 1, c] = next_sweep(here, b1[z + 1, c], around, 1)

    loop(1, 7, later1)

    def last1(z, c):
        here = t1[z, c]
        around = beside(here, rows1, group1) + (t1[z - 1, c] + t1[z + 1, c])
        f1[z - 1, c] = next_sweep(here, b1[z + 2, c], around, 1)

    loop(1, 5, last1)

    rise0 = table(width, half, lambda r, c: r // 2 == c)
    open0 = [
        table(lanes, lanes, lambda r, c, a=a: (r // half == a) & (c // 2 == r % half))
        for a in range(2)
    ]

    def raise0(z1, c):
        coarse = f1[z1, c]
        tall = jnp.concatenate([wide_dot(coarse, open0[0]), wide_dot(coarse, open0[1])], 0)
        up = wide_dot(rise0, tall)
        u0[2 * z1, c] += up
        u0[2 * z1 + 1, c] += up

    loop(0, 4, raise0)

    def later0(z, c):
        here = u0[z, c]
        around = beside(here, width, lanes) + (u0[z - 1, c] + u0[z + 1, c])
        t0[z - 1, c] = next_sweep(here, b0[z + 1, c], around, 0)

    loop(1, 7, later0)

    def last0(z, c):
        here = t0[z, c]
        around = beside(here, width, lanes) + (t0[z - 1, c] + t0[z + 1, c])
        out_ref[z - 1, c] = next_sweep(here, b0[z + 2, c], around, 0)

    loop(1, 5, last0)


def multigrid(source):
    devices = lax.axis_size("gz")
    width = source.shape[3]
    fine, middle, third = (3, width, width), (3, width // 4, width), (3, width // 16, width)
    dma = pltpu.SemaphoreType.DMA
    scratch = [
        pltpu.VMEM((10,) + fine, jnp.float32),
        pltpu.VMEM((8,) + fine, jnp.float32),
        pltpu.VMEM((6,) + fine, jnp.float32),
        pltpu.VMEM((10,) + middle, jnp.float32),
        pltpu.VMEM((8,) + middle, jnp.float32),
        pltpu.VMEM((6,) + middle, jnp.float32),
        pltpu.VMEM((4,) + middle, jnp.float32),
        pltpu.VMEM((devices,) + third, jnp.float32),
        pltpu.VMEM((devices,) + third, jnp.float32),
        dma((4,)),
        dma((4,)),
        dma((4,)),
        dma((4,)),
        dma,
        dma,
    ]
    return pl.pallas_call(
        functools.partial(grid_kernel, devices),
        out_shape=jax.ShapeDtypeStruct(source.shape, jnp.float32),
        in_specs=[VM],
        out_specs=VM,
        scratch_shapes=scratch,
        name="multigrid",
        compiler_params=pltpu.CompilerParams(
            collective_id=0, has_side_effects=True, vmem_limit_bytes=56 * 2**20
        ),
    )(source)


def shards(marker_positions, marker_forces, dest_slab, base_cells, fluid_source):
    devices = lax.axis_size("gz")
    held_blocks = marker_positions.shape[0]
    width = fluid_source.shape[2]
    capacity = max(2, 2 * held_blocks // devices)
    slots = devices * capacity
    target = dest_slab[:, 0]
    earlier = jnp.arange(held_blocks)[:, None] > jnp.arange(held_blocks)[None, :]
    slot_order = jnp.sum((earlier & (target[:, None] == target[None, :])).astype(jnp.int32), axis=1)
    slot_index = target * capacity + slot_order
    tables = marker_tables(marker_positions)
    boxes = pltpu.VMEM((slots, ROWS, 128), jnp.float32)
    grid = pltpu.VMEM((width * ROWS, 128), jnp.float32)
    packed = jax.ShapeDtypeStruct((slots * ROWS, 128), jnp.bfloat16)
    box_sent = local_call(build_kernel, packed, [SM, SM, VM, VM], [boxes], "build")(
        slot_index, base_cells.reshape(-1), tables, marker_forces
    )
    arrived = lax.all_to_all(box_sent, "gz", split_axis=0, concat_axis=0, tiled=True)
    labels = lax.slice(arrived.reshape(slots, ROWS, 128), (0, 0, 0), (slots, 1, 2))
    arrived_base = labels.reshape(-1).astype(jnp.int32)
    source = local_call(
        place_kernel,
        jax.ShapeDtypeStruct(fluid_source.shape, jnp.float32),
        [SM, VM, VM],
        [boxes, grid, grid],
        "place",
    )(arrived_base, arrived, fluid_source)
    velocity = multigrid(source)
    picked = local_call(pick_kernel, packed, [SM, VM], [boxes, grid], "pick")(
        arrived_base, velocity
    )
    returned = lax.all_to_all(picked, "gz", split_axis=0, concat_axis=0, tiled=True)
    marker_velocity = local_call(
        read_kernel,
        jax.ShapeDtypeStruct(marker_positions.shape, jnp.float32),
        [SM, VM, VM],
        [boxes],
        "read",
    )(slot_index, tables, returned)
    return (velocity, marker_velocity)


def solution(mesh):
    placed = (
        P("gz", None, None),
        P("gz", None, None),
        P("gz", None),
        P("gz", None),
        P("gz", None, None, None),
    )
    return jax.shard_map(
        shards,
        mesh=mesh,
        in_specs=placed,
        out_specs=(P("gz", None, None, None), P("gz", None, None)),
        check_vma=False,
    )
```
